32 devices in a mesh: pair: 2 (over y), fsdp: 4 (over x, core), rep: 4 (over z).
Axes of the slice: x: 2, y: 2, z: 4, core: 2. Of those that a mesh axis runs over, the one named last changes fastest.
Arguments:
- tokens: bfloat16 [4096, 2048], P(('pair', 'fsdp', 'rep')), may hold values from -6 to 6
- cotangent: bfloat16 [4096, 2048], P(('pair', 'fsdp', 'rep')), may hold values from -6 to 6
- segment_ids: int32 [4096], P(('pair', 'fsdp', 'rep')), may hold values from 0 to 2, as said below
- positions: int32 [4096], P(('pair', 'fsdp', 'rep')), may hold values from 0 to 381, as said below
- q_weight: bfloat16 [2048, 2048], P('fsdp'), may hold values from -0.4375 to 0.4375
- k_weight: bfloat16 [2048, 512], P('fsdp'), may hold values from -0.4375 to 0.4375
- v_weight: bfloat16 [2048, 512], P('fsdp'), may hold values from -0.5 to 0.5
- o_weight: bfloat16 [2048, 2048], P('fsdp'), may hold values from -1 to 1
- attn_gain: bfloat16 [2048], P('fsdp'), may hold values from 0.5 to 1.5
- gate_up_weight: bfloat16 [2048, 16384], P('fsdp'), may hold values from -0.25 to 0.25
- down_weight: bfloat16 [8192, 2048], P('fsdp'), may hold values from -0.1875 to 0.1875
- mlp_gain: bfloat16 [2048], P('fsdp'), may hold values from 0.5 to 1.5
Outputs:
- out: bfloat16 [4096, 2048], P(('pair', 'fsdp', 'rep'))
- input_grad: bfloat16 [4096, 2048], P(('pair', 'fsdp', 'rep'))
- q_update: float32 [2048, 2048], P(('pair', 'fsdp'))
- k_update: float32 [2048, 512], P(('pair', 'fsdp'))
- v_grad: float32 [2048, 512], P(('pair', 'fsdp'))
- o_grad: float32 [2048, 2048], P(('pair', 'fsdp'))
- attn_gain_grad: float32 [2048], P(('pair', 'fsdp'))
- gate_up_grad: float32 [2048, 16384], P(('pair', 'fsdp'))
- down_grad: float32 [8192, 2048], P(('pair', 'fsdp'))
- mlp_gain_grad: float32 [2048], P(('pair', 'fsdp'))
The draws below stay inside these ranges and needn't reach their ends.
Inputs may be any that keep to these rules, and one draw needn't show every extreme that they name: `segment_ids`: in each group the 128 prompt tokens have segment 0; the 128 continuation tokens fill aligned windows of 128 tokens, each split into two continuations of one token or more, numbered 1 to 2 in order. A group's prompt has consecutive positions from a start below 128; each continuation's positions run consecutively from the prompt's last position plus one.
All inputs are finite; a program needn't handle non-finite values.
Results may differ from the reference program's by a relative error of at most 0.022.
Values may be sent and summed in bfloat16 or wider, within the bound.
No kernel may reach another device: no remote copies, remote signals or barrier semaphores. Data moves between devices by JAX's collectives and lax.ppermute only.
A program may use at most 512 MiB of HBM per device.

```python
import jax
import jax.numpy as jnp
from jax import lax

D = 2048
FF = 8192
HEADS = 32
KV_HEADS = 8
HEAD = 64
PROMPT = 128
CONT = 128
GROUPS = 16
TOKENS = 4096


def group_layout(key):
    base = jax.random.fold_in(key, 11)
    key_cut, key_start = jax.random.split(base)
    windows = PROMPT // CONT
    cut_points = jax.random.randint(key_cut, (GROUPS, windows, 1), 1, CONT)
    cut_points = cut_points.at[1, 0, 0].set(1)
    start_pos = jax.random.randint(key_start, (GROUPS, 1), 0, CONT)
    start_pos = start_pos.at[0, 0].set(0).at[1, 0].set(CONT - 1)
    offset = jnp.arange(CONT, dtype=jnp.int32)[None, None, :]
    second = (offset >= cut_points).astype(jnp.int32)
    window_ids = jnp.arange(windows, dtype=jnp.int32)[None, :, None]
    cont_seg = (2 * window_ids + 1 + second).reshape(GROUPS, PROMPT)
    cont_pos = (offset - second * cut_points).reshape(GROUPS, PROMPT) + start_pos + PROMPT
    prompt_seg = jnp.zeros((GROUPS, PROMPT), jnp.int32)
    prompt_pos = start_pos + jnp.arange(PROMPT, dtype=jnp.int32)[None, :]
    seg_ids = jnp.concatenate([prompt_seg.reshape(-1), cont_seg.reshape(-1)])
    pos_ids = jnp.concatenate([prompt_pos.reshape(-1), cont_pos.reshape(-1)])
    return (seg_ids.astype(jnp.int32), pos_ids.astype(jnp.int32))


def draw_segment_ids(key, part):
    return group_layout(key)[0]


def draw_positions(key, part):
    return group_layout(key)[1]


def level_of(rng, extent, shards, smallest, largest):
    def one(position, shards_of):
        steps = jax.random.uniform(jax.random.fold_in(jax.random.fold_in(rng, 6), position), (shards_of,), jnp.float32, smallest / len(shards), largest / len(shards))
        return jnp.repeat(jnp.exp(steps), extent[position] // shards_of).reshape((-1,) + (1,) * (len(extent) - position - 1))

    level = one(*shards[0])
    for cut in shards[1:]:
        level = level * one(*cut)
    return level


def gaussian(own_key, dims, width, bound, cuts=(), kind=jnp.bfloat16):
    loudness = level_of(own_key, dims, cuts, -0.22, 0.18) if cuts else 1.0
    entries = jax.random.normal(own_key, dims, jnp.float32) * width * loudness
    return jnp.minimum(jnp.maximum(entries, -bound), bound).astype(kind)


def setup_inputs(seed: int = 0) -> dict:
    key_of = jax.random.split(jax.random.key(seed), 13)
    return {
        "tokens": gaussian(key_of[0], (TOKENS, D), 1.0, 6.0, ((0, 32),)),
        "cotangent": gaussian(key_of[1], (TOKENS, D), 1.0, 6.0, ((0, 32),)),
        "segment_ids": draw_segment_ids(jax.random.fold_in(key_of[12], 71), 0),
        "positions": draw_positions(jax.random.fold_in(key_of[12], 71), 0),
        "q_weight": gaussian(key_of[4], (D, D), (D // 12) ** -0.5, 0.4375, ((0, 4),)),
        "k_weight": gaussian(key_of[5], (D, KV_HEADS * HEAD), (D // 12) ** -0.5, 0.4375, ((0, 4),)),
        "v_weight": gaussian(key_of[6], (D, KV_HEADS * HEAD), (D // 16) ** -0.5, 0.5, ((0, 4),)),
        "o_weight": gaussian(key_of[7], (D, D), 32 ** -0.5, 1.0, ((0, 4),)),
        "attn_gain": jnp.clip(1.0 + 0.1 * jax.random.normal(key_of[8], (D,), jnp.float32), 0.5, 1.5).astype(jnp.bfloat16),
        "gate_up_weight": gaussian(key_of[9], (D, 2 * FF), (D // 4) ** -0.5, 0.25, ((0, 4),)),
        "down_weight": gaussian(key_of[10], (FF, D), (FF // 8) ** -0.5, 0.1875, ((0, 4),)),
        "mlp_gain": jnp.clip(1.0 + 0.1 * jax.random.normal(key_of[11], (D,), jnp.float32), 0.5, 1.5).astype(jnp.bfloat16),
    }


@jax.custom_vjp
def low(v):
    return lax.optimization_barrier(v.astype(jnp.bfloat16)).astype(jnp.float32)

@jax.custom_vjp
def low_back(v):
    return v

def low_keep(v):
    return (low(v), None)

def low_pass(kept, grad):
    return (grad,)

def back_keep(v):
    return (v, None)

def back_low(kept, grad):
    return (low(grad),)
low.defvjp(low_keep, low_pass)
low_back.defvjp(back_keep, back_low)
EPS = 1e-05
THETA = 10000000.0
SCALE = 0.015625
RESID = 0.22
TAU = 3.0

def rope_tables(positions, half):
    inverse = THETA ** (-(jnp.arange(half, dtype=jnp.float32) * 2.0 / (2 * half)))
    angle = positions.astype(jnp.float32)[:, None] * inverse[None, :]
    return (jnp.cos(angle), jnp.sin(angle))

def rotate(vectors, cosine, sine, sign):
    half = vectors.shape[-1] // 2
    first = vectors[..., :half]
    second = vectors[..., half:]
    cos_b = cosine[:, None, :]
    sin_b = sign * sine[:, None, :]
    return jnp.concatenate([first * cos_b - second * sin_b, second * cos_b + first * sin_b], axis=-1)

def rms_unit(values):
    return values * lax.rsqrt(lax.optimization_barrier(jnp.mean(values * values, axis=-1, keepdims=True)) + EPS)

def forward_pass(inputs, w_query, w_key, w_value, w_out, gain_attn, w_gate_up, w_down, gain_mlp, segment_ids, positions):
    highest = lax.Precision.HIGHEST
    total_rows = inputs.shape[0]
    half_rows = total_rows // 2
    groups = half_rows // PROMPT
    group_size = HEADS // KV_HEADS
    normed = low(rms_unit(inputs) * gain_attn)
    query_lin = low_back(jnp.dot(normed, w_query, precision=highest))
    key_lin = low_back(jnp.dot(normed, w_key, precision=highest))
    value_all = low(low_back(jnp.dot(normed, w_value, precision=highest)))
    cosine, sine = rope_tables(positions, HEAD // 2)
    query_all = low(rotate(query_lin.reshape(total_rows, HEADS, HEAD), cosine, sine, 1.0))
    key_all = low(rotate(key_lin.reshape(total_rows, KV_HEADS, HEAD), cosine, sine, 1.0))
    value_all = value_all.reshape(total_rows, KV_HEADS, HEAD)

    def by_group(values):
        tail = values.shape[1:]
        return jnp.concatenate([values[:half_rows].reshape((groups, PROMPT) + tail), values[half_rows:].reshape((groups, PROMPT) + tail)], axis=1)

    def attend_group(block):
        query_blk, key_blk, value_blk, seg_blk, pos_blk = block
        seq_len = query_blk.shape[0]
        raw = jnp.einsum('qgjd,kgd->gjqk', query_blk.reshape(seq_len, KV_HEADS, group_size, HEAD), key_blk, precision=highest)
        scores = low_back(raw) * SCALE
        visible = ((seg_blk[None, :] == 0) | (seg_blk[None, :] == seg_blk[:, None])) & (pos_blk[None, :] <= pos_blk[:, None])
        masked = jnp.where(visible[None, None], scores, -jnp.inf)
        peak = lax.optimization_barrier(jnp.max(masked, axis=3, keepdims=True))
        exp_scores = jnp.exp(masked - peak)
        attn_probs = exp_scores / lax.optimization_barrier(jnp.sum(exp_scores, axis=3, keepdims=True))
        mixed = jnp.einsum('gjqk,kgd->qgjd', low(attn_probs), value_blk, precision=highest)
        return (mixed.reshape(seq_len, D), lax.optimization_barrier(jnp.max(masked, axis=(2, 3))).reshape(HEADS))
    attended, tops = lax.map(jax.checkpoint(attend_group), (by_group(query_all), by_group(key_all), by_group(value_all), by_group(segment_ids), by_group(positions)))
    attended = jnp.concatenate([attended[:, :PROMPT].reshape(half_rows, D), attended[:, PROMPT:].reshape(half_rows, D)], axis=0)
    attended = low(low_back(attended))
    branch = low_back(jnp.dot(attended, w_out, precision=highest))
    middle = inputs + RESID * branch
    normed_mlp = low(rms_unit(middle) * gain_mlp)
    gate_up = low_back(jnp.dot(normed_mlp, w_gate_up, precision=highest))
    hidden = low(jax.nn.silu(gate_up[:, :FF]) * gate_up[:, FF:])
    branch_mlp = low_back(jnp.dot(hidden, w_down, precision=highest))
    return (middle + RESID * branch_mlp, lax.optimization_barrier(jnp.max(tops, axis=0)))

def reference(tokens, cotangent, segment_ids, positions, q_weight, k_weight, v_weight, o_weight, attn_gain, gate_up_weight, down_weight, mlp_gain):
    floats = [item.astype(jnp.float32) for item in (tokens, q_weight, k_weight, v_weight, o_weight, attn_gain, gate_up_weight, down_weight, mlp_gain)]

    def wrapped(inputs, w_query, w_key, w_value, w_out, gain_attn, w_gate_up, w_down, gain_mlp):
        return forward_pass(inputs, w_query, w_key, w_value, w_out, gain_attn, w_gate_up, w_down, gain_mlp, segment_ids, positions)
    output, pull, tops = jax.vjp(wrapped, *floats, has_aux=True)
    grads = pull(cotangent.astype(jnp.float32))
    factor = TAU / jnp.maximum(tops, TAU)
    q_factor = jnp.repeat(factor, HEAD)
    k_factor = jnp.repeat(lax.optimization_barrier(jnp.min(factor.reshape(KV_HEADS, HEADS // KV_HEADS), axis=1)), HEAD)
    return (output.astype(jnp.bfloat16), grads[0].astype(jnp.bfloat16), grads[1] * q_factor[None, :], grads[2] * k_factor[None, :], grads[3], grads[4], grads[5], grads[6], grads[7], grads[8])
```

```python
import jax
import jax.numpy as jnp
from jax import lax
from jax.sharding import PartitionSpec as P

D = 2048
FF = 8192
HEADS = 32
KV_HEADS = 8
HEAD = 64
GROUP = HEADS // KV_HEADS

EPS = 1e-05
THETA = 10000000.0
SCALE = 0.015625
RESID = 0.22
TAU = 3.0

PLANE = ("pair", "fsdp")
F32 = jnp.float32
BF16 = jnp.bfloat16
ORDER = (0, 4, 2, 6, 1, 5, 3, 7)


def dot(left, right):
    return jnp.dot(left, right, preferred_element_type=F32)


def outer(left, right):
    return lax.dot_general(left, right, (((0,), (0,)), ((), ())), preferred_element_type=F32)


def times_t(left, right):
    return lax.dot_general(left, right, (((1,), (1,)), ((), ())), preferred_element_type=F32)


def swap(x, mask, devices=8):
    return lax.ppermute(x, PLANE, [(i, i ^ mask) for i in range(devices)])


def rope_tables(positions, half):
    inverse = THETA ** (-(jnp.arange(half, dtype=F32) * 2.0 / (2 * half)))
    angle = positions.astype(F32)[..., None] * inverse
    return (jnp.cos(angle), jnp.sin(angle))


def rotate(vectors, cosine, sine, sign):
    half = vectors.shape[-1] // 2
    first = vectors[..., :half]
    second = vectors[..., half:]
    cos_b = cosine[..., None, :]
    sin_b = sign * sine[..., None, :]
    return jnp.concatenate(
        [first * cos_b - second * sin_b, second * cos_b + first * sin_b], axis=-1
    )


class Plane:
    def __init__(self):
        self.np = lax.axis_size("pair")
        self.nf = lax.axis_size("fsdp")
        self.nr = lax.axis_size("rep")
        self.n = self.np * self.nf
        self.p = lax.axis_index("pair")
        self.f = lax.axis_index("fsdp")
        self.unit = self.np * self.f + self.p
        self.cube = self.np == 2 and self.nf == 4

    def gather(self, x):
        if not self.cube:
            return lax.all_gather(x, PLANE, axis=0, tiled=True)
        near = [x] + [swap(x, m) for m in ORDER[1:4]]
        far = [swap(piece, 1) for piece in near]
        return jnp.concatenate(near + far, axis=0)

    def scatter(self, left, right, product):
        rows = left.shape[0]
        if not self.cube:
            whole = product(left, right).astype(BF16)
            return lax.psum_scatter(whole, PLANE, scatter_dimension=0, tiled=True).astype(F32)
        half = rows // 2
        far = swap(product(left[half:], right).astype(BF16), 1)
        near = product(left[:half], right) + far.astype(F32)
        size = half // 4
        total = near[:size]
        for i in (1, 2, 3):
            piece = near[i * size : (i + 1) * size].astype(BF16)
            total = total + swap(piece, ORDER[i]).astype(F32)
        return total

    def groups(self, x):
        if self.cube:
            return x.reshape((self.nf, -1) + x.shape[1:])
        y = x.reshape((self.np, self.nf, -1) + x.shape[1:])
        return jnp.swapaxes(y, 0, 1).reshape((self.nf, -1) + x.shape[1:])

    def rows(self, x):
        if self.cube:
            return x.reshape((-1,) + x.shape[2:])
        y = x.reshape((self.nf, self.np, -1) + x.shape[2:])
        return jnp.swapaxes(y, 0, 1).reshape((-1,) + x.shape[2:])

    def reshard(self, columns):
        if not self.cube:
            parts = jnp.stack([columns(self.np * i + self.p) for i in range(self.nf)])
            got = lax.all_to_all(parts, "fsdp", 0, 0, tiled=True)
            return got.reshape((-1,) + got.shape[2:])
        own = columns(self.unit)
        rows = own.shape[0]
        out = jnp.zeros((self.nf * rows,) + own.shape[1:], own.dtype)
        out = lax.dynamic_update_slice(out, own, (self.f * rows, 0))
        for k in (1, 2, 3):
            other = self.f ^ k
            got = swap(columns(self.np * other + self.p), k)
            out = lax.dynamic_update_slice(out, got, (other * rows, 0))
        return out

    def by_unit(self, x, axis):
        shape = x.shape
        y = x.reshape(shape[:axis] + (self.np, self.nf) + shape[axis + 1 :])
        return jnp.swapaxes(y, axis, axis + 1).reshape(shape)

    def sum_rows(self, term):
        rows, width = term.shape
        each = rows // (self.n * self.nr)
        split = term.astype(BF16).reshape(self.n, self.nr, each, width)
        mine = lax.psum_scatter(jnp.swapaxes(split, 0, 1), "rep", scatter_dimension=0)
        moved = lax.all_to_all(mine, PLANE, 0, 0, tiled=True)
        full = lax.all_gather(moved, "rep", axis=0)
        return jnp.swapaxes(self.by_unit(full, 1), 1, 2)

    def sum_units(self, term):
        mine = lax.psum_scatter(term.astype(BF16), "rep", scatter_dimension=0, tiled=True)
        pairs = []
        for p in range(self.np):
            for f in range(self.nf):
                pairs.append((p * self.nf + f, self.np * f + p))
        moved = lax.ppermute(mine, PLANE, pairs)
        return lax.all_gather(moved, "rep", axis=0, tiled=True).astype(F32)


def norm_back(grad_normed, unit, inv_scale, gain):
    scaled = grad_normed * gain
    grad_in = inv_scale * (scaled - unit * jnp.mean(scaled * unit, axis=-1, keepdims=True))
    return (grad_in, jnp.sum(grad_normed * unit, axis=0))


def on_device(
    tokens,
    cotangent,
    segment_ids,
    positions,
    q_weight,
    k_weight,
    v_weight,
    o_weight,
    attn_gain,
    gate_up_weight,
    down_weight,
    mlp_gain,
):
    plane = Plane()
    unit, n = plane.unit, plane.n
    heads = HEADS // n
    share = max(1, n // KV_HEADS)
    q_cols = heads * HEAD
    ff = FF // n
    kv_head = unit // share

    def qkv_columns(u):
        rows = q_weight.shape[0]
        return jnp.concatenate(
            [
                lax.dynamic_slice(q_weight, (0, u * q_cols), (rows, q_cols)),
                lax.dynamic_slice(k_weight, (0, (u // share) * HEAD), (rows, HEAD)),
                lax.dynamic_slice(v_weight, (0, (u // share) * HEAD), (rows, HEAD)),
            ],
            axis=1,
        )

    def mlp_columns(u):
        rows = gate_up_weight.shape[0]
        return jnp.concatenate(
            [
                lax.dynamic_slice(gate_up_weight, (0, u * ff), (rows, ff)),
                lax.dynamic_slice(gate_up_weight, (0, FF + u * ff), (rows, ff)),
            ],
            axis=1,
        )

    tokens_all = plane.gather(tokens)
    w_qkv = plane.reshard(qkv_columns)
    gains = lax.all_gather(jnp.stack([attn_gain, mlp_gain]), "fsdp", axis=1, tiled=True)
    gain_one = gains[0].astype(F32)
    gain_two = gains[1].astype(F32)
    segments = plane.groups(plane.gather(segment_ids))
    places = plane.groups(plane.gather(positions))
    w_out = lax.dynamic_slice(o_weight, (plane.p * q_cols, 0), (q_cols, D))
    w_down = lax.dynamic_slice(down_weight, (plane.p * ff, 0), (ff, D))

    inputs_all = tokens_all.astype(F32)
    inv_all = lax.rsqrt(jnp.mean(inputs_all * inputs_all, axis=-1, keepdims=True) + EPS)
    normed = (inputs_all * inv_all * gain_one).astype(BF16)
    lin = dot(normed, w_qkv)
    lin = plane.groups(lin)
    groups, length = lin.shape[:2]
    cosine, sine = rope_tables(places, HEAD // 2)
    query = rotate(lin[..., :q_cols].reshape(groups, length, heads, HEAD), cosine, sine, 1.0)
    query = query.astype(BF16)
    key = rotate(lin[..., None, q_cols : q_cols + HEAD], cosine, sine, 1.0)[:, :, 0].astype(BF16)
    value = lin[..., q_cols + HEAD :].astype(BF16)
    visible = (
        (segments[:, None, :] == 0) | (segments[:, None, :] == segments[:, :, None])
    ) & (places[:, None, :] <= places[:, :, None])
    scores = jnp.einsum("gqjd,gkd->gjqk", query, key, preferred_element_type=F32) * SCALE
    masked = jnp.where(visible[:, None], scores, -jnp.inf)
    peak = jnp.max(masked, axis=3, keepdims=True)
    exp_scores = jnp.exp(masked - peak)
    probs = exp_scores / jnp.sum(exp_scores, axis=3, keepdims=True)
    probs_low = probs.astype(BF16)
    top_local = jnp.max(peak, axis=(0, 2, 3))
    attended = jnp.einsum("gjqk,gkd->gqjd", probs_low, value, preferred_element_type=F32)
    attended = plane.rows(attended.astype(BF16).reshape(groups, length, q_cols))

    inputs = tokens.astype(F32)
    middle = inputs + RESID * plane.scatter(attended, w_out, dot)
    inv_two = lax.rsqrt(jnp.mean(middle * middle, axis=-1, keepdims=True) + EPS)
    unit_two = middle * inv_two
    normed_mlp = plane.gather((unit_two * gain_two).astype(BF16))
    grad_out = cotangent.astype(F32)
    grad_branch = plane.gather((RESID * grad_out).astype(BF16))
    w_gate_up = plane.reshard(mlp_columns)

    gate_up = dot(normed_mlp, w_gate_up)
    gate = gate_up[:, :ff]
    up_part = gate_up[:, ff:]
    sigma = jax.nn.sigmoid(gate)
    silu_gate = gate * sigma
    hidden = (silu_gate * up_part).astype(BF16)
    grad_hidden = times_t(grad_branch, w_down)
    grad_gate_up = jnp.concatenate(
        [grad_hidden * up_part * sigma * (1.0 + gate * (1.0 - sigma)), grad_hidden * silu_gate],
        axis=1,
    ).astype(BF16)
    down_grad = plane.sum_units(outer(hidden, grad_branch))
    grad_normed_mlp = plane.scatter(grad_gate_up, w_gate_up, times_t)
    gate_up_rows = plane.sum_rows(outer(normed_mlp, grad_gate_up))
    owned = gate_up_rows.shape[0] * gate_up_rows.shape[1]
    gate_up_rows = gate_up_rows.reshape(owned, n, 2, ff)
    gate_up_grad = jnp.swapaxes(gate_up_rows, 1, 2).reshape(owned, 2 * FF).astype(F32)
    result = (middle + RESID * plane.scatter(hidden, w_down, dot)).astype(BF16)

    grad_mid_norm, gain_two_grad = norm_back(grad_normed_mlp, unit_two, inv_two, gain_two)
    grad_middle = grad_out + grad_mid_norm
    grad_attn_branch = plane.gather((RESID * grad_middle).astype(BF16))
    grad_attended = times_t(grad_attn_branch, w_out).astype(BF16)
    o_grad = plane.sum_units(outer(attended, grad_attn_branch))
    grad_attended = plane.groups(grad_attended).reshape(groups, length, heads, HEAD)
    grad_probs = jnp.einsum("gqjd,gkd->gjqk", grad_attended, value, preferred_element_type=F32)
    delta = jnp.sum(probs * grad_probs, axis=3, keepdims=True)
    grad_scores = (probs * (grad_probs - delta) * SCALE).astype(BF16)
    grad_query = jnp.einsum("gjqk,gkd->gqjd", grad_scores, key, preferred_element_type=F32)
    grad_key = jnp.einsum("gjqk,gqjd->gkd", grad_scores, query, preferred_element_type=F32)
    grad_value = jnp.einsum("gjqk,gqjd->gkd", probs_low, grad_attended, preferred_element_type=F32)
    grad_query = rotate(grad_query, cosine, sine, -1.0).reshape(groups, length, q_cols)
    grad_key = rotate(grad_key[:, :, None], cosine, sine, -1.0)[:, :, 0]
    grad_lin = plane.rows(
        jnp.concatenate([grad_query, grad_key, grad_value], axis=-1).astype(BF16)
    )
    grad_normed = plane.scatter(grad_lin, w_qkv, times_t)
    lin_rows = plane.sum_rows(outer(normed, grad_lin)).astype(F32)
    inv_one = lax.rsqrt(jnp.mean(inputs * inputs, axis=-1, keepdims=True) + EPS)
    grad_in_norm, gain_one_grad = norm_back(grad_normed, inputs * inv_one, inv_one, gain_one)
    input_grad = (grad_middle + grad_in_norm).astype(BF16)

    lin_rows = lin_rows.reshape((-1,) + lin_rows.shape[2:])
    rows = lin_rows.shape[0]
    tops = jnp.full((HEADS,), -jnp.inf, F32)
    tops = lax.dynamic_update_slice(tops, top_local, (unit * heads,))
    tops = lax.pmax(tops, ("pair", "fsdp", "rep"))
    factor = TAU / jnp.maximum(tops, TAU)
    k_factor = jnp.repeat(jnp.min(factor.reshape(KV_HEADS, GROUP), axis=1), HEAD)
    q_update = lin_rows[..., :q_cols].reshape(rows, D) * jnp.repeat(factor, HEAD)[None, :]
    kv = lin_rows[..., q_cols:].reshape(rows, n // share, share, 2 * HEAD).sum(axis=2)
    k_update = kv[..., :HEAD].reshape(rows, -1) * k_factor[None, :]
    v_grad = kv[..., HEAD:].reshape(rows, -1)
    gain_grads = lax.psum(jnp.stack([gain_one_grad, gain_two_grad]), ("pair", "fsdp", "rep"))
    place = plane.p * plane.nf + plane.f
    gain_grads = lax.dynamic_slice(gain_grads, (0, place * (D // n)), (2, D // n))
    return (
        result,
        input_grad,
        q_update,
        k_update,
        v_grad,
        o_grad,
        gain_grads[0],
        gate_up_grad,
        down_grad,
        gain_grads[1],
    )


def solution(mesh):
    tokens = P(("pair", "fsdp", "rep"))
    shard = P("fsdp")
    owned = P(("pair", "fsdp"))
    return jax.shard_map(
        on_device,
        mesh=mesh,
        in_specs=(tokens,) * 4 + (shard,) * 8,
        out_specs=(tokens, tokens) + (owned,) * 8,
        check_vma=False,
    )
```

```python
import jax
import jax.numpy as jnp
from jax import lax
from jax.experimental import pallas as pl
from jax.experimental.pallas import tpu as pltpu
from jax.sharding import PartitionSpec as P

D = 2048
FF = 8192
HEADS = 32
KV_HEADS = 8
HEAD = 64
GROUP = HEADS // KV_HEADS

EPS = 1e-05
THETA = 10000000.0
SCALE = 0.015625
RESID = 0.22
TAU = 3.0

PLANE = ("pair", "fsdp")
F32 = jnp.float32
BF16 = jnp.bfloat16
ORDER = (0, 4, 2, 6, 1, 5, 3, 7)


def dot(left, right):
    return jnp.dot(left, right, preferred_element_type=F32)


def outer(left, right):
    return lax.dot_general(left, right, (((0,), (0,)), ((), ())), preferred_element_type=F32)


def times_t(left, right):
    return lax.dot_general(left, right, (((1,), (1,)), ((), ())), preferred_element_type=F32)


def swap(x, mask, devices=8):
    return lax.ppermute(x, PLANE, [(i, i ^ mask) for i in range(devices)])


def along(x, pairs):
    return lax.ppermute(x, "rep", pairs)


def after(x, *others):
    return lax.optimization_barrier((x,) + others)[0]


def rope_tables(places, heads):
    half = HEAD // 2
    inverse = THETA ** (-(jnp.arange(half, dtype=F32) * 2.0 / HEAD))
    angle = places.astype(F32)[:, None] * inverse[None, :]
    cosine, sine = jnp.cos(angle), jnp.sin(angle)
    ones, zeros = jnp.ones((places.shape[0], HEAD), F32), jnp.zeros((places.shape[0], HEAD), F32)
    cos_row = jnp.concatenate([cosine] * (2 * heads + 2) + [ones], axis=1)
    sin_row = jnp.concatenate([-sine, sine] * (heads + 1) + [zeros], axis=1)
    return cos_row, sin_row


def half_swap(x):
    width = x.shape[1]
    lane = lax.broadcasted_iota(jnp.int32, x.shape, 1)
    first = (lane & (HEAD - 1)) < HEAD // 2
    return jnp.where(first, pltpu.roll(x, width - HEAD // 2, 1), pltpu.roll(x, HEAD // 2, 1))


def mat_t(left, right):
    return lax.dot_general(left, right, (((1,), (1,)), ((), ())), preferred_element_type=F32)


def mat_tl(left, right):
    return lax.dot_general(left, right, (((0,), (0,)), ((), ())), preferred_element_type=F32)


def attend_kernel(heads, lin_ref, cos_ref, sin_ref, vis_ref, qkv_ref, att_ref, top_ref):
    x = lin_ref[...]
    row = (x * cos_ref[...] + half_swap(x) * sin_ref[...]).astype(BF16)
    qkv_ref[...] = row
    key = row[:, heads * HEAD : (heads + 1) * HEAD]
    value = row[:, (heads + 1) * HEAD :]
    visible = vis_ref[...] > 0.0
    top_ref[...] = jnp.full(top_ref.shape, -jnp.inf, F32)
    outs = []
    for h in range(heads):
        scores = mat_t(row[:, h * HEAD : (h + 1) * HEAD], key) * SCALE
        scores = jnp.where(visible, scores, -jnp.inf)
        peak = jnp.max(scores, axis=1, keepdims=True)
        grown = jnp.exp(scores - peak)
        probs = (grown / jnp.sum(grown, axis=1, keepdims=True)).astype(BF16)
        outs.append(dot(probs, value).astype(BF16))
        top_ref[h : h + 1, :] = jnp.broadcast_to(jnp.max(peak, axis=0, keepdims=True), (1, 128))
    att_ref[...] = jnp.concatenate(outs, axis=1)


def attend_back_kernel(heads, qkv_ref, cos_ref, sin_ref, vis_ref, grad_ref, out_ref):
    row = qkv_ref[...]
    key = row[:, heads * HEAD : (heads + 1) * HEAD]
    value = row[:, (heads + 1) * HEAD :]
    visible = vis_ref[...] > 0.0
    grad_att = grad_ref[...]
    grads = []
    grad_key = jnp.zeros((row.shape[0], HEAD), F32)
    grad_value = jnp.zeros((row.shape[0], HEAD), F32)
    for h in range(heads):
        query = row[:, h * HEAD : (h + 1) * HEAD]
        grad_h = grad_att[:, h * HEAD : (h + 1) * HEAD]
        scores = jnp.where(visible, mat_t(query, key) * SCALE, -jnp.inf)
        peak = jnp.max(scores, axis=1, keepdims=True)
        grown = jnp.exp(scores - peak)
        probs = grown / jnp.sum(grown, axis=1, keepdims=True)
        grad_probs = mat_t(grad_h, value)
        delta = jnp.sum(probs * grad_probs, axis=1, keepdims=True)
        grad_scores = (probs * (grad_probs - delta) * SCALE).astype(BF16)
        grads.append(dot(grad_scores, key))
        grad_key = grad_key + mat_tl(grad_scores, query)
        grad_value = grad_value + mat_tl(probs.astype(BF16), grad_h)
    x = jnp.concatenate(grads + [grad_key, grad_value], axis=1)
    out_ref[...] = (x * cos_ref[...] - half_swap(x) * sin_ref[...]).astype(BF16)


def by_group(kernel, heads, length, ins, outs, name, flops):
    groups = ins[0].shape[0] // length

    def spec(x):
        rows = x.shape[0] // groups
        return pl.BlockSpec((rows, x.shape[1]), lambda g: (g, 0))

    return pl.pallas_call(
        lambda *refs: kernel(heads, *refs),
        grid=(groups,),
        in_specs=[spec(x) for x in ins],
        out_specs=[spec(x) for x in outs],
        out_shape=outs,
        name=name,
        cost_estimate=pl.CostEstimate(
            flops=flops, bytes_accessed=4 * sum(x.size for x in ins), transcendentals=0
        ),
    )(*ins)


def place_kernel(count, table, *refs):
    which = table[0, pl.program_id(0)]
    out_ref = refs[-1]
    for b in range(count):

        @pl.when(which == b)
        def _():
            out_ref[...] = refs[b][0].astype(F32)


def place(shards, table, shape, into, name):
    _, rows, columns = shards[0].shape
    count = len(shards)
    steps = table.shape[1]

    def pick(b):
        return pl.BlockSpec((1, rows, columns), lambda i, t: (t[1 + b, i], 0, 0))

    in_specs = [pick(b) for b in range(count)]
    args = list(shards)
    aliases = {}
    if into is not None:
        in_specs.append(pl.BlockSpec(memory_space=pl.ANY))
        args.append(into)
        aliases = {1 + count: 0}
    return pl.pallas_call(
        lambda t, *refs: place_kernel(count, t, *refs),
        grid_spec=pltpu.PrefetchScalarGridSpec(
            num_scalar_prefetch=1,
            grid=(steps,),
            in_specs=in_specs,
            out_specs=pl.BlockSpec((rows, columns), lambda i, t: (t[1 + count, i], t[2 + count, i])),
        ),
        out_shape=jax.ShapeDtypeStruct(shape, F32),
        input_output_aliases=aliases,
        name=name,
        cost_estimate=pl.CostEstimate(
            flops=0, bytes_accessed=6 * steps * rows * columns, transcendentals=0
        ),
    )(table, *args)


class Plane:
    def __init__(self):
        self.np = lax.axis_size("pair")
        self.nf = lax.axis_size("fsdp")
        self.nr = lax.axis_size("rep")
        self.n = self.np * self.nf
        self.p = lax.axis_index("pair")
        self.f = lax.axis_index("fsdp")
        self.z = lax.axis_index("rep")
        self.place = self.p * self.nf + self.f
        self.unit = self.np * self.f + self.p
        self.cube = self.np == 2 and self.nf == 4
        self.line = self.nr == 4

    def gather(self, x, axis=0):
        if not self.cube:
            full = lax.all_gather(x, PLANE, axis=axis, tiled=True)
            return self.to_groups(full, axis)
        near = [x] + [swap(x, m) for m in ORDER[1:4]]
        far = [swap(piece, 1) for piece in near]
        return jnp.concatenate(near + far, axis=axis)

    def gather_x_first(self, x):
        if not self.cube:
            return self.gather(x)
        two = jnp.stack([x, swap(x, 2)])
        other = swap(two, 4)
        near = [two[0], other[0], two[1], other[1]]
        two_far, other_far = swap(two, 1), swap(other, 1)
        far = [two_far[0], other_far[0], two_far[1], other_far[1]]
        return jnp.concatenate(near + far, axis=0)

    def to_groups(self, x, axis=0):
        shape = x.shape
        y = x.reshape(shape[:axis] + (self.np, self.nf, -1) + shape[axis + 1 :])
        return jnp.swapaxes(y, axis, axis + 1).reshape(shape)

    def from_groups(self, x):
        y = x.reshape((self.nf, self.np, -1) + x.shape[1:])
        return jnp.swapaxes(y, 0, 1).reshape(x.shape)

    def scatter(self, left, right, product):
        rows = left.shape[0]
        if not self.cube:
            whole = self.from_groups(product(left, right).astype(BF16))
            return lax.psum_scatter(whole, PLANE, scatter_dimension=0, tiled=True).astype(F32)
        half = rows // 2
        far = swap(product(left[half:], right).astype(BF16), 1)
        near = product(left[:half], right) + far.astype(F32)
        size = half // 4
        total = near[:size]
        for i in (1, 2, 3):
            piece = near[i * size : (i + 1) * size].astype(BF16)
            total = total + swap(piece, ORDER[i]).astype(F32)
        return total

    def reshard(self, columns):
        if not self.cube:
            parts = jnp.stack([columns(self.np * i + self.p) for i in range(self.nf)])
            got = lax.all_to_all(parts, "fsdp", 0, 0, tiled=True)
            return got.reshape((-1,) + got.shape[2:])
        own = columns(self.unit)
        rows = own.shape[0]
        out = jnp.zeros((self.nf * rows,) + own.shape[1:], own.dtype)
        out = lax.dynamic_update_slice(out, own, (self.f * rows, 0))
        for k in (1, 2, 3):
            other = self.f ^ k
            got = swap(columns(self.np * other + self.p), k)
            out = lax.dynamic_update_slice(out, got, (other * rows, 0))
        return out

    def reshard_shared(self, columns, first):
        if not (self.cube and self.line):
            return self.reshard(columns)
        own = columns(self.unit)
        rows, width = own.shape
        quarter = rows // 4
        out = jnp.zeros((self.nf * rows, width), own.dtype)
        out = lax.dynamic_update_slice(out, own, (self.f * rows, 0))
        near = swap(columns(self.np * (self.f ^ 1) + self.p), 1)
        out = lax.dynamic_update_slice(out, near, ((self.f ^ 1) * rows, 0))
        got = []
        for k in (2, 3):
            piece = columns(self.np * (self.f ^ k) + self.p)
            piece = lax.dynamic_slice(piece, (self.z * quarter, 0), (quarter, width))
            got.append(swap(after(piece, *first), k))
        shards = self.line_gather(jnp.stack(got))
        for shard, where in zip(shards[::-1], self.line_shards()[::-1]):
            for i, k in enumerate((2, 3)):
                start = (self.f ^ k) * rows + where * quarter
                out = lax.dynamic_update_slice(out, shard[i], (start, 0))
        return out

    def line_shards(self):
        z = self.z
        return (
            z,
            jnp.maximum(z - 1, 0),
            jnp.minimum(z + 1, 3),
            jnp.where(z < 2, z + 2, z - 2),
            jnp.where(z == 0, 3, jnp.where(z == 3, 0, z)),
        )

    def line_gather(self, own):
        right = along(own, [(0, 1), (1, 2), (2, 3)])
        left = along(own, [(1, 0), (2, 1), (3, 2)])
        two = jnp.where(
            self.z < 2, along(left, [(1, 0), (2, 1)]), along(right, [(1, 2), (2, 3)])
        )
        three = along(two, [(2, 3), (1, 0)])
        return (own, right, left, two, three)

    def line_scatter(self, part):
        z = self.z

        def plus(i, *others):
            total = part(i).astype(F32)
            for other in others:
                total = total + other.astype(F32)
            return total.astype(BF16)

        three = along(plus(jnp.where(z == 0, 3, 0)), [(0, 1), (3, 2)])
        two = plus(jnp.where(z < 2, z + 2, z - 2), three)
        right = along(two, [(0, 1), (1, 2)])
        left = along(two, [(2, 1), (3, 2)])
        right = along(plus(jnp.minimum(z + 1, 3), right), [(0, 1), (1, 2), (2, 3)])
        left = along(plus(jnp.maximum(z - 1, 0), left), [(1, 0), (2, 1), (3, 2)])
        return plus(z, right, left)

    def table(self, blocks, rows_of, columns_of):
        z = self.z
        shard = jnp.repeat(jnp.arange(4), blocks)
        block = jnp.tile(jnp.arange(blocks), 4)
        apart = jnp.abs(shard - z)
        which = jnp.where(apart == 0, 0, jnp.where(apart == 1, jnp.where(shard < z, 1, 2), apart + 1))
        rows = [which]
        for b, held in enumerate(self.line_shards()):
            idle = jnp.where(shard > held, blocks - 1, 0)
            rows.append(jnp.where(which == b, block, idle))
        rows.append(rows_of(shard, block))
        rows.append(columns_of(shard, block))
        return jnp.stack([jnp.broadcast_to(r, shard.shape).astype(jnp.int32) for r in rows])

    def unit_of(self, place):
        return self.np * (place % self.nf) + place // self.nf

    def exchange(self, mine):
        if not self.cube:
            moved = lax.all_to_all(mine, PLANE, 0, 0, tiled=True)
            return moved, self.unit_of(jnp.arange(self.n))
        got = []
        for m in range(8):
            piece = lax.dynamic_index_in_dim(mine, self.place ^ m, 0, keepdims=False)
            got.append(swap(piece, m) if m else piece)
        return jnp.stack(got), self.unit_of(self.place ^ jnp.arange(8))

    def to_owner(self, x):
        pairs = []
        for p in range(self.np):
            for f in range(self.nf):
                pairs.append((p * self.nf + f, self.np * f + p))
        return lax.ppermute(x, PLANE, pairs)

    def sum_rows(self, term):
        rows, width = term.shape
        each = rows // (self.n * self.nr)
        split = term.astype(BF16).reshape(self.n, self.nr, each, width)
        if self.line:
            mine = self.line_scatter(lambda i: lax.dynamic_index_in_dim(split, i, 1, keepdims=False))
            moved, units = self.exchange(mine)
            return self.line_gather(moved), units
        mine = lax.psum_scatter(jnp.swapaxes(split, 0, 1), "rep", scatter_dimension=0)
        moved, units = self.exchange(mine)
        return lax.all_gather(moved, "rep", axis=0), units

    def sum_rows_full(self, term):
        shards, units = self.sum_rows(term)
        if self.line:
            full = jnp.zeros((4,) + shards[0].shape, BF16)
            for shard, where in zip(shards[::-1], self.line_shards()[::-1]):
                full = lax.dynamic_update_slice(full, shard[None], (where, 0, 0, 0))
        else:
            full = shards
        inverse = jnp.zeros((self.n,), jnp.int32).at[units].set(jnp.arange(self.n, dtype=jnp.int32))
        full = jnp.swapaxes(jnp.take(full, inverse, axis=1), 1, 2)
        return full.reshape((-1,) + full.shape[2:])

    def sum_units(self, term, name):
        rows, width = term.shape
        low = term.astype(BF16)
        if not self.line:
            mine = lax.psum_scatter(low, "rep", scatter_dimension=0, tiled=True)
            return lax.all_gather(self.to_owner(mine), "rep", axis=0, tiled=True).astype(F32)
        split = low.reshape(4, rows // 4, width)
        mine = self.line_scatter(lambda i: lax.dynamic_index_in_dim(split, i, 0, keepdims=False))
        shards = self.line_gather(self.to_owner(mine))
        table = self.table(1, lambda s, b: s, lambda s, b: 0)
        return place([x[None] for x in shards], table, (rows, width), None, name)

    def sum_gate_up(self, gate_term, up_term):
        ff = gate_term.shape[1]
        if not self.line:
            both = []
            for term in (gate_term, up_term):
                full = self.sum_rows_full(term)
                both.append(full.reshape(full.shape[0], -1))
            return jnp.concatenate(both, axis=1).astype(F32)
        out = None
        for i, term in enumerate((gate_term, up_term)):
            shards, units = self.sum_rows(term)
            table = self.table(
                self.n, lambda s, b: s, lambda s, b: i * self.n + jnp.take(units, b)
            )
            shape = (term.shape[0] // self.n, 2 * self.n * ff)
            out = place(shards, table, shape, out, "place_gate_up")
        return out

    def total(self, sums, top):
        if not (self.cube and self.line):
            everyone = ("pair", "fsdp", "rep")
            return lax.psum(sums, everyone), lax.pmax(top, everyone)
        count = sums.shape[0]
        both = jnp.concatenate([sums, top], axis=0)

        def join(a, b):
            return jnp.concatenate(
                [a[:count] + b[:count], jnp.maximum(a[count:], b[count:])], axis=0
            )

        for m in (1, 2, 4):
            both = join(both, swap(both, m))
        ends = [(0, 1), (3, 2)]
        inner = (self.z == 1) | (self.z == 2)
        both = jnp.where(inner, join(both, along(both, ends)), both)
        both = join(both, along(both, [(1, 2), (2, 1)]))
        both = jnp.where(inner, both, along(both, [(1, 0), (2, 3)]))
        return both[:count], both[count:]


def norm_back(grad_normed, unit, inv_scale, gain):
    scaled = grad_normed * gain
    grad_in = inv_scale * (scaled - unit * jnp.mean(scaled * unit, axis=-1, keepdims=True))
    return (grad_in, jnp.sum(grad_normed * unit, axis=0))


def on_device(
    tokens,
    cotangent,
    segment_ids,
    positions,
    q_weight,
    k_weight,
    v_weight,
    o_weight,
    attn_gain,
    gate_up_weight,
    down_weight,
    mlp_gain,
):
    plane = Plane()
    unit, n = plane.unit, plane.n
    heads = HEADS // n
    share = max(1, n // KV_HEADS)
    q_cols = heads * HEAD
    ff = FF // n
    length = plane.np * tokens.shape[0]

    def qkv_columns(u):
        rows = q_weight.shape[0]
        return jnp.concatenate(
            [
                lax.dynamic_slice(q_weight, (0, u * q_cols), (rows, q_cols)),
                lax.dynamic_slice(k_weight, (0, (u // share) * HEAD), (rows, HEAD)),
                lax.dynamic_slice(v_weight, (0, (u // share) * HEAD), (rows, HEAD)),
            ],
            axis=1,
        )

    def mlp_columns(u):
        rows = gate_up_weight.shape[0]
        return jnp.concatenate(
            [
                lax.dynamic_slice(gate_up_weight, (0, u * ff), (rows, ff)),
                lax.dynamic_slice(gate_up_weight, (0, FF + u * ff), (rows, ff)),
            ],
            axis=1,
        )

    tokens_all = plane.gather_x_first(tokens)
    w_qkv = plane.reshard(qkv_columns)
    gains = lax.all_gather(jnp.stack([attn_gain, mlp_gain]), "fsdp", axis=1, tiled=True)
    gain_one = gains[0].astype(F32)
    gain_two = gains[1].astype(F32)
    where = plane.gather(jnp.stack([segment_ids, positions]), axis=1)
    segments = where[0].reshape(-1, length)
    places = where[1].reshape(-1, length)
    visible = (
        (segments[:, None, :] == 0) | (segments[:, None, :] == segments[:, :, None])
    ) & (places[:, None, :] <= places[:, :, None])
    visible = visible.astype(F32).reshape(-1, length)
    cosine, sine = rope_tables(places.reshape(-1), heads)
    w_out = lax.dynamic_slice(o_weight, (plane.p * q_cols, 0), (q_cols, D))
    w_down = lax.dynamic_slice(down_weight, (plane.p * ff, 0), (ff, D))

    inputs_all = tokens_all.astype(F32)
    inv_all = lax.rsqrt(jnp.mean(inputs_all * inputs_all, axis=-1, keepdims=True) + EPS)
    normed = (inputs_all * inv_all * gain_one).astype(BF16)
    lin = dot(normed, w_qkv)
    count = lin.shape[0]
    flops = 4 * count * length * HEAD * heads
    qkv, attended, tops = by_group(
        attend_kernel,
        heads,
        length,
        [lin, cosine, sine, visible],
        [
            jax.ShapeDtypeStruct(lin.shape, BF16),
            jax.ShapeDtypeStruct((count, q_cols), BF16),
            jax.ShapeDtypeStruct((8 * (count // length), 128), F32),
        ],
        "attend",
        flops,
    )

    w_gate_up = plane.reshard_shared(mlp_columns, (tokens_all, w_qkv))
    grad_out = cotangent.astype(F32)
    low_out = after((RESID * grad_out).astype(BF16), tokens_all)
    grad_branch = plane.gather_x_first(low_out)
    grad_hidden = times_t(grad_branch, w_down)

    inputs = tokens.astype(F32)
    middle = inputs + RESID * plane.scatter(attended, w_out, dot)
    inv_two = lax.rsqrt(jnp.mean(middle * middle, axis=-1, keepdims=True) + EPS)
    unit_two = middle * inv_two
    normed_mlp = plane.gather((unit_two * gain_two).astype(BF16))

    gate_up = dot(normed_mlp, w_gate_up)
    gate = gate_up[:, :ff]
    up_part = gate_up[:, ff:]
    sigma = jax.nn.sigmoid(gate)
    silu_gate = gate * sigma
    hidden = (silu_gate * up_part).astype(BF16)
    grad_gate = (grad_hidden * up_part * sigma * (1.0 + gate * (1.0 - sigma))).astype(BF16)
    grad_up = (grad_hidden * silu_gate).astype(BF16)
    grad_gate_up = jnp.concatenate([grad_gate, grad_up], axis=1)
    down_grad = plane.sum_units(outer(hidden, grad_branch), "place_down")
    gate_up_grad = plane.sum_gate_up(outer(normed_mlp, grad_gate), outer(normed_mlp, grad_up))
    grad_normed_mlp = plane.scatter(grad_gate_up, w_gate_up, times_t)
    result = (middle + RESID * plane.scatter(hidden, w_down, dot)).astype(BF16)

    grad_mid_norm, gain_two_grad = norm_back(grad_normed_mlp, unit_two, inv_two, gain_two)
    grad_middle = grad_out + grad_mid_norm
    grad_attn_branch = plane.gather((RESID * grad_middle).astype(BF16))
    grad_attended = times_t(grad_attn_branch, w_out).astype(BF16)
    o_grad = plane.sum_units(outer(attended, grad_attn_branch), "place_o")
    (grad_lin,) = by_group(
        attend_back_kernel,
        heads,
        length,
        [qkv, cosine, sine, visible, grad_attended],
        [jax.ShapeDtypeStruct(lin.shape, BF16)],
        "attend_back",
        3 * flops,
    )
    grad_normed = plane.scatter(grad_lin, w_qkv, times_t)
    lin_rows = plane.sum_rows_full(outer(normed, grad_lin)).astype(F32)
    inv_one = lax.rsqrt(jnp.mean(inputs * inputs, axis=-1, keepdims=True) + EPS)
    grad_in_norm, gain_one_grad = norm_back(grad_normed, inputs * inv_one, inv_one, gain_one)
    input_grad = (grad_middle + grad_in_norm).astype(BF16)

    top_local = jnp.max(tops.reshape(-1, 8, 128), axis=(0, 2))[:heads]
    top_row = jnp.full((1, D), -jnp.inf, F32)
    top_row = lax.dynamic_update_slice(top_row, top_local[None], (0, unit * heads))
    gain_grads, top_row = plane.total(jnp.stack([gain_one_grad, gain_two_grad]), top_row)
    factor = TAU / jnp.maximum(top_row[0, :HEADS], TAU)
    k_factor = jnp.repeat(jnp.min(factor.reshape(KV_HEADS, GROUP), axis=1), HEAD)
    rows = lin_rows.shape[0]
    q_update = lin_rows[..., :q_cols].reshape(rows, D) * jnp.repeat(factor, HEAD)[None, :]
    kv = lin_rows[..., q_cols:].reshape(rows, n // share, share, 2 * HEAD).sum(axis=2)
    k_update = kv[..., :HEAD].reshape(rows, -1) * k_factor[None, :]
    v_grad = kv[..., HEAD:].reshape(rows, -1)
    gain_grads = lax.dynamic_slice(gain_grads, (0, plane.place * (D // n)), (2, D // n))
    return (
        result,
        input_grad,
        q_update,
        k_update,
        v_grad,
        o_grad,
        gain_grads[0],
        gate_up_grad,
        down_grad,
        gain_grads[1],
    )


def solution(mesh):
    tokens = P(("pair", "fsdp", "rep"))
    shard = P("fsdp")
    owned = P(("pair", "fsdp"))
    return jax.shard_map(
        on_device,
        mesh=mesh,
        in_specs=(tokens,) * 4 + (shard,) * 8,
        out_specs=(tokens, tokens) + (owned,) * 8,
        check_vma=False,
    )
```

```python
import jax
import jax.numpy as jnp
from jax import lax
from jax.experimental import pallas as pl
from jax.experimental.pallas import tpu as pltpu
from jax.sharding import PartitionSpec as P

D = 2048
FF = 8192
HEADS = 32
KV_HEADS = 8
HEAD = 64
GROUP = HEADS // KV_HEADS

EPS = 1e-05
THETA = 10000000.0
SCALE = 0.015625
RESID = 0.22
TAU = 3.0

PLANE = ("pair", "fsdp")
F32 = jnp.float32
BF16 = jnp.bfloat16
ORDER = (0, 4, 2, 6, 1, 5, 3, 7)


def dot(left, right):
    return jnp.dot(left, right, preferred_element_type=F32)


def outer(left, right):
    return lax.dot_general(left, right, (((0,), (0,)), ((), ())), preferred_element_type=F32)


def times_t(left, right):
    return lax.dot_general(left, right, (((1,), (1,)), ((), ())), preferred_element_type=F32)


def swap(x, mask, devices=8):
    return lax.ppermute(x, PLANE, [(i, i ^ mask) for i in range(devices)])


def along(x, pairs):
    return lax.ppermute(x, "rep", pairs)


def after(x, *others):
    return lax.optimization_barrier((x,) + others)[0]


def rope_tables(places):
    half = HEAD // 2
    lane = jnp.arange(2 * HEAD)
    inverse = THETA ** (-((lane % half).astype(F32) * 2.0 / HEAD))
    angle = places.astype(F32)[:, None] * inverse[None, :]
    sign = jnp.where(lane % HEAD < half, -1.0, 1.0)
    return jnp.cos(angle), jnp.sin(angle) * sign[None, :]


def whole_row(cos, sin, heads):
    turned = lax.broadcasted_iota(jnp.int32, cos.shape, 1) < HEAD
    pairs = heads // 2
    cos_row = jnp.concatenate([cos] * pairs + [jnp.where(turned, cos, 1.0)], axis=1)
    sin_row = jnp.concatenate([sin] * pairs + [jnp.where(turned, sin, 0.0)], axis=1)
    return cos_row, sin_row


def half_swap(x):
    width = x.shape[1]
    lane = lax.broadcasted_iota(jnp.int32, x.shape, 1)
    first = (lane & (HEAD - 1)) < HEAD // 2
    return jnp.where(first, pltpu.roll(x, width - HEAD // 2, 1), pltpu.roll(x, HEAD // 2, 1))


def mat_t(left, right):
    return lax.dot_general(left, right, (((1,), (1,)), ((), ())), preferred_element_type=F32)


def mat_tl(left, right):
    return lax.dot_general(left, right, (((0,), (0,)), ((), ())), preferred_element_type=F32)


def attend_kernel(
    heads,
    near,
    first_near,
    second_near,
    first_far,
    second_far,
    gain_ref,
    weight_ref,
    cos_ref,
    sin_ref,
    vis_ref,
    normed_ref,
    qkv_ref,
    att_ref,
    top_ref,
    tokens_ref,
):
    rows = first_near.shape[1]

    @pl.when(pl.program_id(0) < near)
    def _():
        tokens_ref[:rows] = first_near[0]
        tokens_ref[rows:] = second_near[0]

    @pl.when(pl.program_id(0) >= near)
    def _():
        tokens_ref[:rows] = first_far[0]
        tokens_ref[rows:] = second_far[0]

    inputs = tokens_ref[...].astype(F32)
    inv = lax.rsqrt(jnp.mean(inputs * inputs, axis=1, keepdims=True) + EPS)
    normed = (inputs * inv * gain_ref[...]).astype(BF16)
    normed_ref[...] = normed
    x = dot(normed, weight_ref[...])
    cos_row, sin_row = whole_row(cos_ref[...], sin_ref[...], heads)
    row = (x * cos_row + half_swap(x) * sin_row).astype(BF16)
    qkv_ref[...] = row
    key = row[:, heads * HEAD : (heads + 1) * HEAD]
    value = row[:, (heads + 1) * HEAD :]
    visible = vis_ref[...] > 0.0
    top_ref[...] = jnp.full(top_ref.shape, -jnp.inf, F32)
    outs = []
    for h in range(heads):
        scores = mat_t(row[:, h * HEAD : (h + 1) * HEAD], key) * SCALE
        scores = jnp.where(visible, scores, -jnp.inf)
        peak = jnp.max(scores, axis=1, keepdims=True)
        grown = jnp.exp(scores - peak)
        probs = (grown / jnp.sum(grown, axis=1, keepdims=True)).astype(BF16)
        outs.append(dot(probs, value).astype(BF16))
        top_ref[h : h + 1, :] = jnp.broadcast_to(jnp.max(peak, axis=0, keepdims=True), (1, 128))
    att_ref[...] = jnp.concatenate(outs, axis=1)


def attend(heads, parts, gain, weight, cosine, sine, visible):
    near = parts[0].shape[0]
    groups = near + parts[2].shape[0]
    length = parts[0].shape[1] + parts[1].shape[1]
    width = weight.shape[1]

    def part(x, is_near):
        block = (1,) + x.shape[1:]
        if is_near:
            return pl.BlockSpec(block, lambda g: (jnp.minimum(g, near - 1), 0, 0))
        return pl.BlockSpec(block, lambda g: (jnp.maximum(g - near, 0), 0, 0))

    def whole(x):
        return pl.BlockSpec(x.shape, lambda g: (0, 0))

    def rows(columns, each=length):
        return pl.BlockSpec((each, columns), lambda g: (g, 0))

    total = groups * length
    return pl.pallas_call(
        lambda *refs: attend_kernel(heads, near, *refs),
        grid=(groups,),
        in_specs=[part(x, i < 2) for i, x in enumerate(parts)]
        + [whole(gain), whole(weight), rows(cosine.shape[1]), rows(sine.shape[1]), rows(visible.shape[1])],
        out_specs=[rows(D), rows(width), rows(heads * HEAD), rows(128, 8)],
        out_shape=[
            jax.ShapeDtypeStruct((total, D), BF16),
            jax.ShapeDtypeStruct((total, width), BF16),
            jax.ShapeDtypeStruct((total, heads * HEAD), BF16),
            jax.ShapeDtypeStruct((8 * groups, 128), F32),
        ],
        scratch_shapes=[pltpu.VMEM((length, D), BF16)],
        name="attend",
        cost_estimate=pl.CostEstimate(
            flops=2 * total * D * width, bytes_accessed=8 * total * D, transcendentals=0
        ),
    )(*parts, gain, weight, cosine, sine, visible)


def attend_back_kernel(heads, qkv_ref, cos_ref, sin_ref, vis_ref, grad_ref, out_ref):
    row = qkv_ref[...]
    key = row[:, heads * HEAD : (heads + 1) * HEAD]
    value = row[:, (heads + 1) * HEAD :]
    visible = vis_ref[...] > 0.0
    grad_att = grad_ref[...]
    grads = []
    grad_key = jnp.zeros((row.shape[0], HEAD), F32)
    grad_value = jnp.zeros((row.shape[0], HEAD), F32)
    for h in range(heads):
        query = row[:, h * HEAD : (h + 1) * HEAD]
        grad_h = grad_att[:, h * HEAD : (h + 1) * HEAD]
        scores = jnp.where(visible, mat_t(query, key) * SCALE, -jnp.inf)
        peak = jnp.max(scores, axis=1, keepdims=True)
        grown = jnp.exp(scores - peak)
        probs = grown / jnp.sum(grown, axis=1, keepdims=True)
        grad_probs = mat_t(grad_h, value)
        delta = jnp.sum(probs * grad_probs, axis=1, keepdims=True)
        grad_scores = (probs * (grad_probs - delta) * SCALE).astype(BF16)
        grads.append(dot(grad_scores, key))
        grad_key = grad_key + mat_tl(grad_scores, query)
        grad_value = grad_value + mat_tl(probs.astype(BF16), grad_h)
    x = jnp.concatenate(grads + [grad_key, grad_value], axis=1)
    cos_row, sin_row = whole_row(cos_ref[...], sin_ref[...], heads)
    out_ref[...] = (x * cos_row - half_swap(x) * sin_row).astype(BF16)


def per_group(kernel, heads, length, ins, outs, name, flops):
    groups = ins[0].shape[0] // length

    def spec(x):
        rows = x.shape[0] // groups
        return pl.BlockSpec((rows, x.shape[1]), lambda g: (g, 0))

    return pl.pallas_call(
        lambda *refs: kernel(heads, *refs),
        grid=(groups,),
        in_specs=[spec(x) for x in ins],
        out_specs=[spec(x) for x in outs],
        out_shape=outs,
        name=name,
        cost_estimate=pl.CostEstimate(
            flops=flops, bytes_accessed=4 * sum(x.size for x in ins), transcendentals=0
        ),
    )(*ins)


def place_kernel(table, sum_ref, copy_ref, *refs):
    out_ref = refs[-1]

    @pl.when(table[0] == 1)
    def _():
        out_ref[...] = sum_ref[...].astype(F32)

    @pl.when(table[0] == 0)
    def _():
        out_ref[...] = copy_ref[...].astype(F32)


def place(table, summed, copied, into, shape, name):
    rows, width = summed.shape
    half = rows // 2
    columns = width // 2
    piece = pl.BlockSpec((half, columns), lambda i, j, t: (j, i))
    in_specs = [piece, piece]
    args = [summed, copied]
    aliases = {}
    if into is not None:
        in_specs.append(pl.BlockSpec(memory_space=pl.ANY))
        args.append(into)
        aliases = {3: 0}
    return pl.pallas_call(
        place_kernel,
        grid_spec=pltpu.PrefetchScalarGridSpec(
            num_scalar_prefetch=1,
            grid=(2, 2),
            in_specs=in_specs,
            out_specs=pl.BlockSpec((half, columns), lambda i, j, t: (j, t[1 + i])),
        ),
        out_shape=jax.ShapeDtypeStruct(shape, F32),
        input_output_aliases=aliases,
        name=name,
        cost_estimate=pl.CostEstimate(flops=0, bytes_accessed=8 * rows * width, transcendentals=0),
    )(table, *args)


class Line:
    def __init__(self, z):
        self.inner = (z == 1) | (z == 2)
        self.rounds = ([], [], [])

    def send(self, stage, x, pairs):
        sent = self.rounds[stage]
        if len(sent) >= 2:
            x = after(x, sent[-2])
        sent.append(along(x, pairs))
        return x, sent[-1]

    def sum(self, x):
        x, more = self.send(0, x, [(0, 1), (3, 2)])
        x, more = self.send(1, x + more, [(1, 2), (2, 1)])
        return self.send(2, x + more, [(1, 0), (2, 3)])

    def pick(self, summed, copied):
        return jnp.where(self.inner, summed, copied)


class Plane:
    def __init__(self):
        self.np = lax.axis_size("pair")
        self.nf = lax.axis_size("fsdp")
        self.nr = lax.axis_size("rep")
        self.n = self.np * self.nf
        self.p = lax.axis_index("pair")
        self.f = lax.axis_index("fsdp")
        self.z = lax.axis_index("rep")
        self.place = self.p * self.nf + self.f
        self.unit = self.np * self.f + self.p
        self.cube = self.np == 2 and self.nf == 4
        self.line = self.nr == 4

    def gather(self, x, axis=0):
        if not self.cube:
            full = lax.all_gather(x, PLANE, axis=axis, tiled=True)
            return self.to_groups(full, axis)
        near = [x] + [swap(x, m) for m in ORDER[1:4]]
        far = [swap(piece, 1) for piece in near]
        return jnp.concatenate(near + far, axis=axis)

    def gather_parts(self, x, swapped, hold=()):
        two = jnp.stack([x, swapped])
        other = swap(after(two, *hold), 4)
        return two, other, swap(two, 1), swap(other, 1)

    def gather_small(self, x):
        pair = jnp.concatenate([x, swap(x, 4)], axis=1)
        quad = jnp.concatenate([pair, swap(pair, 2)], axis=1)
        return jnp.concatenate([quad, swap(quad, 1)], axis=1)

    def gather_gains(self, x):
        for k in (1, 2):
            other = swap(x, k)
            odd = (self.f & k) > 0
            x = jnp.concatenate([jnp.where(odd, other, x), jnp.where(odd, x, other)], axis=1)
        return x

    def to_groups(self, x, axis=0):
        shape = x.shape
        y = x.reshape(shape[:axis] + (self.np, self.nf, -1) + shape[axis + 1 :])
        return jnp.swapaxes(y, axis, axis + 1).reshape(shape)

    def from_groups(self, x):
        y = x.reshape((self.nf, self.np, -1) + x.shape[1:])
        return jnp.swapaxes(y, 0, 1).reshape(x.shape)

    def scatter(self, left, right, product):
        rows = left.shape[0]
        if not self.cube:
            whole = self.from_groups(product(left, right).astype(BF16))
            total = lax.psum_scatter(whole, PLANE, scatter_dimension=0, tiled=True).astype(F32)
            return total, whole
        half = rows // 2
        far = swap(product(left[half:], right).astype(BF16), 1)
        near = product(left[:half], right) + far.astype(F32)
        size = half // 4
        total = near[:size]
        pieces = [near[i * size : (i + 1) * size].astype(BF16) for i in (1, 2, 3)]
        for i, piece in enumerate(pieces):
            total = total + swap(piece, ORDER[i + 1]).astype(F32)
        return total, pieces[0]

    def reshard(self, columns):
        if not self.cube:
            parts = jnp.stack([columns(self.np * i + self.p) for i in range(self.nf)])
            got = lax.all_to_all(parts, "fsdp", 0, 0, tiled=True)
            return got.reshape((-1,) + got.shape[2:]), ()
        own = columns(self.unit)
        rows = own.shape[0]
        got = [swap(columns(self.np * (self.f ^ k) + self.p), k) for k in (1, 2, 3)]
        out = jnp.zeros((self.nf * rows,) + own.shape[1:], own.dtype)
        out = lax.dynamic_update_slice(out, own, (self.f * rows, 0))
        for k, piece in zip((1, 2, 3), got):
            out = lax.dynamic_update_slice(out, piece, ((self.f ^ k) * rows, 0))
        return out, tuple(got[1:])

    def reshard_shared(self, columns, first):
        own = columns(self.unit, 0, 1)
        rows, width = own.shape
        half = rows // 2
        part = self.z & 1
        near = swap(columns(self.np * (self.f ^ 1) + self.p, 0, 1), 1)
        got = []
        for k in (2, 3):
            piece = columns(self.np * (self.f ^ k) + self.p, part, 2)
            got.append(swap(after(piece, *first, *got), k))

        def finish(hold):
            out = jnp.zeros((self.nf * rows, width), own.dtype)
            out = lax.dynamic_update_slice(out, own, (self.f * rows, 0))
            out = lax.dynamic_update_slice(out, near, ((self.f ^ 1) * rows, 0))
            for k, piece in zip((2, 3), got):
                start = (self.f ^ k) * rows
                other = along(after(piece, hold), [(0, 1), (1, 0), (2, 3), (3, 2)])
                out = lax.dynamic_update_slice(out, piece, (start + part * half, 0))
                out = lax.dynamic_update_slice(out, other, (start + (1 - part) * half, 0))
            return out

        return finish

    def unit_of(self, place):
        return self.np * (place % self.nf) + place // self.nf

    def to_owner(self, x):
        pairs = []
        for p in range(self.np):
            for f in range(self.nf):
                pairs.append((p * self.nf + f, self.np * f + p))
        return lax.ppermute(x, PLANE, pairs)

    def sum_rows(self, term):
        rows, width = term.shape
        each = rows // (self.n * self.nr)
        split = term.astype(BF16).reshape(self.n, self.nr, each, width)
        mine = lax.psum_scatter(jnp.swapaxes(split, 0, 1), "rep", scatter_dimension=0)
        moved = lax.all_to_all(mine, PLANE, 0, 0, tiled=True)
        full = jnp.swapaxes(lax.all_gather(moved, "rep", axis=0), 0, 1)
        return full.reshape(self.n, -1, width), self.unit_of(jnp.arange(self.n))

    def in_order(self, full, units):
        inverse = jnp.zeros((self.n,), jnp.int32).at[units].set(jnp.arange(self.n, dtype=jnp.int32))
        return jnp.swapaxes(jnp.take(full, inverse, axis=0), 0, 1)

    def sum_units(self, term):
        mine = lax.psum_scatter(term.astype(BF16), "rep", scatter_dimension=0, tiled=True)
        return lax.all_gather(self.to_owner(mine), "rep", axis=0, tiled=True)

    def block_for(self, split, m):
        return lax.dynamic_index_in_dim(split, self.place ^ m, 0, keepdims=False)

    def exchange(self, split):
        order = jnp.take(split, self.place ^ jnp.arange(8), axis=0)
        near = order[0::2]
        far = swap(order[1::2], 1)
        both = [jnp.stack([near[j], far[j]]) for j in range(4)]
        return jnp.concatenate([both[0]] + [swap(both[j], 2 * j) for j in (1, 2, 3)], axis=0)

    def total(self, sums, top):
        if not (self.cube and self.line):
            everyone = ("pair", "fsdp", "rep")
            return lax.psum(sums, everyone), lax.pmax(top, everyone)
        count = sums.shape[0]
        both = jnp.concatenate([sums, top], axis=0)

        def join(a, b):
            return jnp.concatenate(
                [a[:count] + b[:count], jnp.maximum(a[count:], b[count:])], axis=0
            )

        for m in (1, 2, 4):
            both = join(both, swap(both, m))
        ends = [(0, 1), (3, 2)]
        inner = (self.z == 1) | (self.z == 2)
        both = jnp.where(inner, join(both, along(both, ends)), both)
        both = join(both, along(both, [(1, 2), (2, 1)]))
        both = jnp.where(inner, both, along(both, [(1, 0), (2, 3)]))
        return both[:count], both[count:]


def norm_back(grad_normed, unit, inv_scale, gain):
    scaled = grad_normed * gain
    grad_in = inv_scale * (scaled - unit * jnp.mean(scaled * unit, axis=-1, keepdims=True))
    return (grad_in, jnp.sum(grad_normed * unit, axis=0))


def on_device(
    tokens,
    cotangent,
    segment_ids,
    positions,
    q_weight,
    k_weight,
    v_weight,
    o_weight,
    attn_gain,
    gate_up_weight,
    down_weight,
    mlp_gain,
):
    plane = Plane()
    fast = plane.cube and plane.line
    unit, n = plane.unit, plane.n
    heads = HEADS // n
    share = max(1, n // KV_HEADS)
    q_cols = heads * HEAD
    ff = FF // n
    length = plane.np * tokens.shape[0]

    def qkv_columns(u):
        rows = q_weight.shape[0]
        return jnp.concatenate(
            [
                lax.dynamic_slice(q_weight, (0, u * q_cols), (rows, q_cols)),
                lax.dynamic_slice(k_weight, (0, (u // share) * HEAD), (rows, HEAD)),
                lax.dynamic_slice(v_weight, (0, (u // share) * HEAD), (rows, HEAD)),
            ],
            axis=1,
        )

    def mlp_columns(u, part=0, parts=1):
        rows = gate_up_weight.shape[0] // parts
        return jnp.concatenate(
            [
                lax.dynamic_slice(gate_up_weight, (part * rows, u * ff), (rows, ff)),
                lax.dynamic_slice(gate_up_weight, (part * rows, FF + u * ff), (rows, ff)),
            ],
            axis=1,
        )

    grad_out = cotangent.astype(F32)
    low_out = (RESID * grad_out).astype(BF16)
    gains = jnp.stack([attn_gain, mlp_gain])
    where = jnp.stack([segment_ids, positions])
    w_out = lax.dynamic_slice(o_weight, (plane.p * q_cols, 0), (q_cols, D))
    w_down = lax.dynamic_slice(down_weight, (plane.p * ff, 0), (ff, D))
    if fast:
        crossed = swap(tokens, 2)
        parts = plane.gather_parts(tokens, crossed)
        where = plane.gather_small(where)
        gains = plane.gather_gains(gains)
        w_qkv, arrived = plane.reshard(qkv_columns)
        finish_gate_up = plane.reshard_shared(mlp_columns, (crossed,) + arrived)
        low_crossed = swap(after(low_out, crossed), 2)
        low_parts = plane.gather_parts(low_out, low_crossed, (parts[1],))
        grad_branch = jnp.concatenate(
            [low_parts[i][j] for i, j in ((0, 0), (1, 0), (0, 1), (1, 1), (2, 0), (3, 0), (2, 1), (3, 1))], axis=0
        )
    else:
        by_group = plane.gather(tokens).reshape(-1, 2, length // 2, D)
        near = by_group.shape[0] // 2
        parts = [by_group[:near, 0], by_group[:near, 1], by_group[near:, 0], by_group[near:, 1]]
        where = plane.gather(where, axis=1)
        gains = lax.all_gather(gains, "fsdp", axis=1, tiled=True)
        w_qkv, _ = plane.reshard(qkv_columns)
        w_gate_up, _ = plane.reshard(mlp_columns)
        grad_branch = plane.gather(low_out)
    gain_one = gains[0].astype(F32)
    gain_two = gains[1].astype(F32)
    segments = where[0].reshape(-1, length)
    places = where[1].reshape(-1, length)
    visible = (
        (segments[:, None, :] == 0) | (segments[:, None, :] == segments[:, :, None])
    ) & (places[:, None, :] <= places[:, :, None])
    visible = visible.astype(F32).reshape(-1, length)
    cosine, sine = rope_tables(places.reshape(-1))

    normed, qkv, attended, tops = attend(
        heads, parts, gain_one[None], w_qkv, cosine, sine, visible
    )
    count = qkv.shape[0]
    flops = 4 * count * length * HEAD * heads

    inputs = tokens.astype(F32)
    branch, sent = plane.scatter(attended, w_out, dot)
    if fast:
        w_gate_up = finish_gate_up(sent)
    middle = inputs + RESID * branch
    inv_two = lax.rsqrt(jnp.mean(middle * middle, axis=-1, keepdims=True) + EPS)
    unit_two = middle * inv_two
    low_two = (unit_two * gain_two).astype(BF16)
    normed_mlp = plane.gather(low_two)
    grad_hidden = lax.optimization_barrier(times_t(grad_branch, w_down))

    gate = lax.optimization_barrier(dot(normed_mlp, w_gate_up[:, :ff]))
    up_part = dot(normed_mlp, w_gate_up[:, ff:])
    sigma = jax.nn.sigmoid(gate)
    silu_gate = gate * sigma
    hidden = (silu_gate * up_part).astype(BF16)
    grad_gate = (grad_hidden * up_part * sigma * (1.0 + gate * (1.0 - sigma))).astype(BF16)
    grad_up = (grad_hidden * silu_gate).astype(BF16)
    grad_gate_up = jnp.concatenate([grad_gate, grad_up], axis=1)

    def back(grad_normed_mlp):
        grad_mid_norm, gain_two_grad = norm_back(grad_normed_mlp, unit_two, inv_two, gain_two)
        grad_middle = grad_out + grad_mid_norm
        grad_attn_branch = plane.gather((RESID * grad_middle).astype(BF16))
        grad_attended = times_t(grad_attn_branch, w_out).astype(BF16)
        (grad_lin,) = per_group(
            attend_back_kernel,
            heads,
            length,
            [qkv, cosine, sine, visible, grad_attended],
            [jax.ShapeDtypeStruct(qkv.shape, BF16)],
            "attend_back",
            3 * flops,
        )
        return grad_middle, grad_attn_branch, grad_lin, gain_two_grad

    rows = D // n
    shape = (rows, 2 * FF)
    if fast:
        line = Line(plane.z)
        each = ff // 4
        downs = [
            outer(hidden[:, i * each : (i + 1) * each], grad_branch).astype(BF16) for i in range(4)
        ]
        grad_gate_up = after(grad_gate_up, *downs)
        downs = [line.sum(x) for x in downs]
        grad_normed_mlp, sent = plane.scatter(grad_gate_up, w_gate_up, times_t)
        term = outer(after(normed_mlp, sent), grad_gate_up).astype(BF16).reshape(n, rows, 2 * ff)
        blocks = {0: plane.block_for(term, 0), 1: swap(plane.block_for(term, 1), 1)}
        hold = (grad_normed_mlp,)
        for pair in ((2, 4), (3, 5), (6,), (7,)):
            for m in pair:
                blocks[m] = swap(after(plane.block_for(term, m), *hold), m)
            hold = tuple(blocks[m] for m in pair)
        grad_middle, grad_attn_branch, grad_lin, gain_two_grad = back(grad_normed_mlp)
        o_term = outer(attended, grad_attn_branch).astype(BF16)
        branch, _ = plane.scatter(after(hidden, grad_attn_branch), w_down, dot)
        grad_normed, _ = plane.scatter(grad_lin, w_qkv, times_t)
        lin_term = plane.exchange(outer(normed, grad_lin).astype(BF16).reshape(n, rows, -1))
        gate_up_grad = None

        def put(m, into):
            u = plane.unit_of(plane.place ^ m)
            table = jnp.stack([line.inner.astype(jnp.int32), u, n + u])
            return place(table, *line.sum(blocks[m]), into, shape, "place_gate_up")

        for m in (0, 1, 2, 4, 3, 5, 6):
            gate_up_grad = put(m, gate_up_grad)
        o_grad = plane.to_owner(line.pick(*line.sum(o_term))).astype(F32)
        lin_rows = line.pick(*line.sum(lin_term))
        lin_units = plane.unit_of(plane.place ^ jnp.arange(8))
        gate_up_grad = put(7, gate_up_grad)
        down_grad = jnp.concatenate(
            [plane.to_owner(line.pick(*x)).astype(F32) for x in downs], axis=0
        )
    else:
        down_grad = plane.sum_units(outer(hidden, grad_branch)).astype(F32)
        full, units = plane.sum_rows(outer(normed_mlp, grad_gate_up))
        full = plane.in_order(full, units).reshape(rows, n, 2, ff)
        gate_up_grad = jnp.swapaxes(full, 1, 2).reshape(shape).astype(F32)
        grad_normed_mlp, _ = plane.scatter(grad_gate_up, w_gate_up, times_t)
        grad_middle, grad_attn_branch, grad_lin, gain_two_grad = back(grad_normed_mlp)
        branch, _ = plane.scatter(hidden, w_down, dot)
        grad_normed, _ = plane.scatter(grad_lin, w_qkv, times_t)
        o_grad = plane.sum_units(outer(attended, grad_attn_branch)).astype(F32)
        lin_rows, lin_units = plane.sum_rows(outer(normed, grad_lin))

    result = (middle + RESID * branch).astype(BF16)
    inv_one = lax.rsqrt(jnp.mean(inputs * inputs, axis=-1, keepdims=True) + EPS)
    grad_in_norm, gain_one_grad = norm_back(grad_normed, inputs * inv_one, inv_one, gain_one)
    input_grad = (grad_middle + grad_in_norm).astype(BF16)

    top_local = jnp.max(tops.reshape(-1, 8, 128), axis=(0, 2))[:heads]
    top_row = jnp.full((1, D), -jnp.inf, F32)
    top_row = lax.dynamic_update_slice(top_row, top_local[None], (0, unit * heads))
    gain_grads, top_row = plane.total(jnp.stack([gain_one_grad, gain_two_grad]), top_row)
    factor = TAU / jnp.maximum(top_row[0, :HEADS], TAU)
    k_factor = jnp.repeat(jnp.min(factor.reshape(KV_HEADS, GROUP), axis=1), HEAD)
    lin_rows = plane.in_order(lin_rows, lin_units).astype(F32)
    q_update = lin_rows[..., :q_cols].reshape(rows, D) * jnp.repeat(factor, HEAD)[None, :]
    kv = lin_rows[..., q_cols:].reshape(rows, n // share, share, 2 * HEAD).sum(axis=2)
    k_update = kv[..., :HEAD].reshape(rows, -1) * k_factor[None, :]
    v_grad = kv[..., HEAD:].reshape(rows, -1)
    gain_grads = lax.dynamic_slice(gain_grads, (0, plane.place * rows), (2, rows))
    return (
        result,
        input_grad,
        q_update,
        k_update,
        v_grad,
        o_grad,
        gain_grads[0],
        gate_up_grad,
        down_grad,
        gain_grads[1],
    )


def solution(mesh):
    tokens = P(("pair", "fsdp", "rep"))
    shard = P("fsdp")
    owned = P(("pair", "fsdp"))
    return jax.shard_map(
        on_device,
        mesh=mesh,
        in_specs=(tokens,) * 4 + (shard,) * 8,
        out_specs=(tokens, tokens) + (owned,) * 8,
        check_vma=False,
    )
```

```python
import jax
import jax.numpy as jnp
from jax import lax
from jax.experimental import pallas as pl
from jax.experimental.pallas import tpu as pltpu
from jax.sharding import PartitionSpec as P

D = 2048
FF = 8192
HEADS = 32
KV_HEADS = 8
HEAD = 64
GROUP = HEADS // KV_HEADS

EPS = 1e-05
THETA = 10000000.0
SCALE = 0.015625
RESID = 0.22
TAU = 3.0

PLANE = ("pair", "fsdp")
F32 = jnp.float32
BF16 = jnp.bfloat16
ORDER = (0, 4, 2, 6, 1, 5, 3, 7)


def dot(left, right):
    return jnp.dot(left, right, preferred_element_type=F32)


def outer(left, right):
    return lax.dot_general(left, right, (((0,), (0,)), ((), ())), preferred_element_type=F32)


def times_t(left, right):
    return lax.dot_general(left, right, (((1,), (1,)), ((), ())), preferred_element_type=F32)


def swap(x, mask, devices=8):
    return lax.ppermute(x, PLANE, [(i, i ^ mask) for i in range(devices)])


def along(x, pairs):
    return lax.ppermute(x, "rep", pairs)


def after(x, *others):
    return lax.optimization_barrier((x,) + others)[0]


def rope_tables(places):
    half = HEAD // 2
    lane = jnp.arange(2 * HEAD)
    inverse = THETA ** (-((lane % half).astype(F32) * 2.0 / HEAD))
    angle = places.astype(F32)[:, None] * inverse[None, :]
    sign = jnp.where(lane % HEAD < half, -1.0, 1.0)
    return jnp.cos(angle), jnp.sin(angle) * sign[None, :]


def whole_row(cos, sin, heads):
    turned = lax.broadcasted_iota(jnp.int32, cos.shape, 1) < HEAD
    pairs = heads // 2
    cos_row = jnp.concatenate([cos] * pairs + [jnp.where(turned, cos, 1.0)], axis=1)
    sin_row = jnp.concatenate([sin] * pairs + [jnp.where(turned, sin, 0.0)], axis=1)
    return cos_row, sin_row


def half_swap(x):
    width = x.shape[1]
    lane = lax.broadcasted_iota(jnp.int32, x.shape, 1)
    first = (lane & (HEAD - 1)) < HEAD // 2
    return jnp.where(first, pltpu.roll(x, width - HEAD // 2, 1), pltpu.roll(x, HEAD // 2, 1))


def mat_t(left, right):
    return lax.dot_general(left, right, (((1,), (1,)), ((), ())), preferred_element_type=F32)


def mat_tl(left, right):
    return lax.dot_general(left, right, (((0,), (0,)), ((), ())), preferred_element_type=F32)


def attend_kernel(
    heads,
    near,
    first_near,
    second_near,
    first_far,
    second_far,
    gain_ref,
    weight_ref,
    cos_ref,
    sin_ref,
    vis_ref,
    normed_ref,
    qkv_ref,
    att_ref,
    top_ref,
    tokens_ref,
):
    rows = first_near.shape[1]

    @pl.when(pl.program_id(0) < near)
    def _():
        tokens_ref[:rows] = first_near[0]
        tokens_ref[rows:] = second_near[0]

    @pl.when(pl.program_id(0) >= near)
    def _():
        tokens_ref[:rows] = first_far[0]
        tokens_ref[rows:] = second_far[0]

    inputs = tokens_ref[...].astype(F32)
    inv = lax.rsqrt(jnp.mean(inputs * inputs, axis=1, keepdims=True) + EPS)
    normed = (inputs * inv * gain_ref[...]).astype(BF16)
    normed_ref[...] = normed
    x = dot(normed, weight_ref[...])
    cos_row, sin_row = whole_row(cos_ref[...], sin_ref[...], heads)
    row = (x * cos_row + half_swap(x) * sin_row).astype(BF16)
    qkv_ref[...] = row
    key = row[:, heads * HEAD : (heads + 1) * HEAD]
    value = row[:, (heads + 1) * HEAD :]
    visible = vis_ref[...] > 0.0
    top_ref[...] = jnp.full(top_ref.shape, -jnp.inf, F32)
    outs = []
    for h in range(heads):
        scores = mat_t(row[:, h * HEAD : (h + 1) * HEAD], key) * SCALE
        scores = jnp.where(visible, scores, -jnp.inf)
        peak = jnp.max(scores, axis=1, keepdims=True)
        grown = jnp.exp(scores - peak)
        probs = (grown / jnp.sum(grown, axis=1, keepdims=True)).astype(BF16)
        outs.append(dot(probs, value).astype(BF16))
        top_ref[h : h + 1, :] = jnp.broadcast_to(jnp.max(peak, axis=0, keepdims=True), (1, 128))
    att_ref[...] = jnp.concatenate(outs, axis=1)


def attend(heads, parts, gain, weight, cosine, sine, visible):
    near = parts[0].shape[0]
    groups = near + parts[2].shape[0]
    length = parts[0].shape[1] + parts[1].shape[1]
    width = weight.shape[1]

    def part(x, is_near):
        block = (1,) + x.shape[1:]
        if is_near:
            return pl.BlockSpec(block, lambda g: (jnp.minimum(g, near - 1), 0, 0))
        return pl.BlockSpec(block, lambda g: (jnp.maximum(g - near, 0), 0, 0))

    def whole(x):
        return pl.BlockSpec(x.shape, lambda g: (0, 0))

    def rows(columns, each=length):
        return pl.BlockSpec((each, columns), lambda g: (g, 0))

    total = groups * length
    return pl.pallas_call(
        lambda *refs: attend_kernel(heads, near, *refs),
        grid=(groups,),
        in_specs=[part(x, i < 2) for i, x in enumerate(parts)]
        + [whole(gain), whole(weight), rows(cosine.shape[1]), rows(sine.shape[1]), rows(visible.shape[1])],
        out_specs=[rows(D), rows(width), rows(heads * HEAD), rows(128, 8)],
        out_shape=[
            jax.ShapeDtypeStruct((total, D), BF16),
            jax.ShapeDtypeStruct((total, width), BF16),
            jax.ShapeDtypeStruct((total, heads * HEAD), BF16),
            jax.ShapeDtypeStruct((8 * groups, 128), F32),
        ],
        scratch_shapes=[pltpu.VMEM((length, D), BF16)],
        name="attend",
        cost_estimate=pl.CostEstimate(
            flops=2 * total * D * width, bytes_accessed=8 * total * D, transcendentals=0
        ),
    )(*parts, gain, weight, cosine, sine, visible)


def attend_back_kernel(heads, qkv_ref, cos_ref, sin_ref, vis_ref, grad_ref, out_ref):
    row = qkv_ref[...]
    key = row[:, heads * HEAD : (heads + 1) * HEAD]
    value = row[:, (heads + 1) * HEAD :]
    visible = vis_ref[...] > 0.0
    grad_att = grad_ref[...]
    grads = []
    grad_key = jnp.zeros((row.shape[0], HEAD), F32)
    grad_value = jnp.zeros((row.shape[0], HEAD), F32)
    for h in range(heads):
        query = row[:, h * HEAD : (h + 1) * HEAD]
        grad_h = grad_att[:, h * HEAD : (h + 1) * HEAD]
        scores = jnp.where(visible, mat_t(query, key) * SCALE, -jnp.inf)
        peak = jnp.max(scores, axis=1, keepdims=True)
        grown = jnp.exp(scores - peak)
        probs = grown / jnp.sum(grown, axis=1, keepdims=True)
        grad_probs = mat_t(grad_h, value)
        delta = jnp.sum(probs * grad_probs, axis=1, keepdims=True)
        grad_scores = (probs * (grad_probs - delta) * SCALE).astype(BF16)
        grads.append(dot(grad_scores, key))
        grad_key = grad_key + mat_tl(grad_scores, query)
        grad_value = grad_value + mat_tl(probs.astype(BF16), grad_h)
    x = jnp.concatenate(grads + [grad_key, grad_value], axis=1)
    cos_row, sin_row = whole_row(cos_ref[...], sin_ref[...], heads)
    out_ref[...] = (x * cos_row - half_swap(x) * sin_row).astype(BF16)


def per_group(kernel, heads, length, ins, outs, name, flops):
    groups = ins[0].shape[0] // length

    def spec(x):
        rows = x.shape[0] // groups
        return pl.BlockSpec((rows, x.shape[1]), lambda g: (g, 0))

    return pl.pallas_call(
        lambda *refs: kernel(heads, *refs),
        grid=(groups,),
        in_specs=[spec(x) for x in ins],
        out_specs=[spec(x) for x in outs],
        out_shape=outs,
        name=name,
        cost_estimate=pl.CostEstimate(
            flops=flops, bytes_accessed=4 * sum(x.size for x in ins), transcendentals=0
        ),
    )(*ins)


def place_kernel(table, sum_ref, copy_ref, *refs):
    out_ref = refs[-1]

    @pl.when(table[0] == 1)
    def _():
        out_ref[...] = sum_ref[...].astype(F32)

    @pl.when(table[0] == 0)
    def _():
        out_ref[...] = copy_ref[...].astype(F32)


def place(table, summed, copied, into, shape, name):
    rows, width = summed.shape
    half = rows // 2
    columns = width // 2
    piece = pl.BlockSpec((half, columns), lambda i, j, t: (j, i))
    in_specs = [piece, piece]
    args = [summed, copied]
    aliases = {}
    if into is not None:
        in_specs.append(pl.BlockSpec(memory_space=pl.ANY))
        args.append(into)
        aliases = {3: 0}
    return pl.pallas_call(
        place_kernel,
        grid_spec=pltpu.PrefetchScalarGridSpec(
            num_scalar_prefetch=1,
            grid=(2, 2),
            in_specs=in_specs,
            out_specs=pl.BlockSpec((half, columns), lambda i, j, t: (j, t[1 + i])),
        ),
        out_shape=jax.ShapeDtypeStruct(shape, F32),
        input_output_aliases=aliases,
        name=name,
        cost_estimate=pl.CostEstimate(flops=0, bytes_accessed=8 * rows * width, transcendentals=0),
    )(table, *args)


class Clock:
    def __init__(self):
        self.kept = []
        self.before = ()

    def start(self, x):
        return after(x, *self.before) if self.before else x

    def keep(self, x):
        self.kept.append(x)
        return x

    def next(self):
        self.before, self.kept = tuple(self.kept), []


class Line:
    def __init__(self, clock, z):
        self.clock = clock
        self.inner = (z == 1) | (z == 2)
        self.across = None
        self.back = None

    def send(self, x, pairs):
        x = self.clock.start(x)
        return x, self.clock.keep(along(x, pairs))

    def step(self, x=None):
        done = None
        chunk, middle, self.across = x, self.across, None
        if chunk is not None:
            chunk, more = self.send(chunk, [(0, 1), (3, 2)])
            self.across = chunk + more
        if self.back is not None:
            done = self.send(self.back, [(1, 0), (2, 3)])
            self.back = None
        if middle is not None:
            middle, more = self.send(middle, [(1, 2), (2, 1)])
            self.back = middle + more
        return done

    def pick(self, summed, copied):
        return jnp.where(self.inner, summed, copied)


class Plane:
    def __init__(self):
        self.np = lax.axis_size("pair")
        self.nf = lax.axis_size("fsdp")
        self.nr = lax.axis_size("rep")
        self.n = self.np * self.nf
        self.p = lax.axis_index("pair")
        self.f = lax.axis_index("fsdp")
        self.z = lax.axis_index("rep")
        self.place = self.p * self.nf + self.f
        self.unit = self.np * self.f + self.p
        self.cube = self.np == 2 and self.nf == 4
        self.line = self.nr == 4

    def gather(self, x, axis=0):
        if not self.cube:
            full = lax.all_gather(x, PLANE, axis=axis, tiled=True)
            return self.to_groups(full, axis)
        near = [x] + [swap(x, m) for m in ORDER[1:4]]
        far = [swap(piece, 1) for piece in near]
        return jnp.concatenate(near + far, axis=axis)

    def gather_parts(self, x, swapped, hold=()):
        two = jnp.stack([x, swapped])
        other = swap(after(two, *hold), 4)
        return two, other, swap(two, 1), swap(other, 1)

    def gather_small(self, x):
        pair = jnp.concatenate([x, swap(x, 4)], axis=1)
        quad = jnp.concatenate([pair, swap(pair, 2)], axis=1)
        return jnp.concatenate([quad, swap(quad, 1)], axis=1)

    def gather_gains(self, x):
        for k in (1, 2):
            other = swap(x, k)
            odd = (self.f & k) > 0
            x = jnp.concatenate([jnp.where(odd, other, x), jnp.where(odd, x, other)], axis=1)
        return x

    def to_groups(self, x, axis=0):
        shape = x.shape
        y = x.reshape(shape[:axis] + (self.np, self.nf, -1) + shape[axis + 1 :])
        return jnp.swapaxes(y, axis, axis + 1).reshape(shape)

    def from_groups(self, x):
        y = x.reshape((self.nf, self.np, -1) + x.shape[1:])
        return jnp.swapaxes(y, 0, 1).reshape(x.shape)

    def scatter(self, left, right, product):
        if not self.cube:
            whole = self.from_groups(product(left, right).astype(BF16))
            return lax.psum_scatter(whole, PLANE, scatter_dimension=0, tiled=True).astype(F32)
        return self.close(*self.near_half(left, right, product, self.far_half(left, right, product)))

    def far_half(self, left, right, product):
        return swap(product(left[left.shape[0] // 2 :], right).astype(BF16), 1)

    def near_half(self, left, right, product, far):
        half = left.shape[0] // 2
        size = half // 4
        near = product(left[:half], right) + far.astype(F32)
        return near[:size], [near[i * size : (i + 1) * size].astype(BF16) for i in (1, 2, 3)]

    def close(self, total, pieces, clock=None):
        got = []
        for i, piece in enumerate(pieces):
            got.append(swap(clock.start(piece) if clock else piece, ORDER[i + 1]))
        for piece in got:
            if clock:
                clock.keep(piece)
            total = total + piece.astype(F32)
        return total

    def reshard(self, columns):
        if not self.cube:
            parts = jnp.stack([columns(self.np * i + self.p) for i in range(self.nf)])
            got = lax.all_to_all(parts, "fsdp", 0, 0, tiled=True)
            return got.reshape((-1,) + got.shape[2:]), ()
        own = columns(self.unit)
        rows = own.shape[0]
        got = [swap(columns(self.np * (self.f ^ k) + self.p), k) for k in (1, 2, 3)]
        out = jnp.zeros((self.nf * rows,) + own.shape[1:], own.dtype)
        out = lax.dynamic_update_slice(out, own, (self.f * rows, 0))
        for k, piece in zip((1, 2, 3), got):
            out = lax.dynamic_update_slice(out, piece, ((self.f ^ k) * rows, 0))
        return out, tuple(got[1:])

    def reshard_shared(self, columns, first):
        part = self.z & 1
        got = []
        for k in (2, 3):
            piece = columns(self.np * (self.f ^ k) + self.p, part, 2)
            got.append(swap(after(piece, *first), k))

        def finish(hold):
            zero = after(jnp.zeros((), BF16), hold)
            own = columns(after(self.unit, hold), 0, 1)
            rows, width = own.shape
            half = rows // 2
            near = swap(columns(after(self.np * (self.f ^ 1) + self.p, hold), 0, 1), 1)
            out = jnp.broadcast_to(zero, (self.nf * rows, width))
            out = lax.dynamic_update_slice(out, own, (self.f * rows, 0))
            out = lax.dynamic_update_slice(out, near, ((self.f ^ 1) * rows, 0))
            for k, piece in zip((2, 3), got):
                start = (self.f ^ k) * rows
                other = along(after(piece, hold), [(0, 1), (1, 0), (2, 3), (3, 2)])
                out = lax.dynamic_update_slice(out, piece, (start + part * half, 0))
                out = lax.dynamic_update_slice(out, other, (start + (1 - part) * half, 0))
            return out

        return finish

    def unit_of(self, place):
        return self.np * (place % self.nf) + place // self.nf

    def to_owner(self, x):
        pairs = []
        for p in range(self.np):
            for f in range(self.nf):
                pairs.append((p * self.nf + f, self.np * f + p))
        return lax.ppermute(x, PLANE, pairs)

    def sum_rows(self, term):
        rows, width = term.shape
        each = rows // (self.n * self.nr)
        split = term.astype(BF16).reshape(self.n, self.nr, each, width)
        mine = lax.psum_scatter(jnp.swapaxes(split, 0, 1), "rep", scatter_dimension=0)
        moved = lax.all_to_all(mine, PLANE, 0, 0, tiled=True)
        full = jnp.swapaxes(lax.all_gather(moved, "rep", axis=0), 0, 1)
        return full.reshape(self.n, -1, width), self.unit_of(jnp.arange(self.n))

    def in_order(self, full, units):
        inverse = jnp.zeros((self.n,), jnp.int32).at[units].set(jnp.arange(self.n, dtype=jnp.int32))
        return jnp.swapaxes(jnp.take(full, inverse, axis=0), 0, 1)

    def sum_units(self, term):
        mine = lax.psum_scatter(term.astype(BF16), "rep", scatter_dimension=0, tiled=True)
        return lax.all_gather(self.to_owner(mine), "rep", axis=0, tiled=True)

    def block_for(self, split, m):
        return lax.dynamic_index_in_dim(split, self.place ^ m, 0, keepdims=False)

    def total(self, sums, top):
        count = sums.shape[0]
        both = jnp.concatenate([sums, top], axis=0)

        def join(a, b):
            return jnp.concatenate(
                [a[:count] + b[:count], jnp.maximum(a[count:], b[count:])], axis=0
            )

        for m in (1, 2, 4):
            both = join(both, swap(both, m))
            yield both
        inner = (self.z == 1) | (self.z == 2)
        both = jnp.where(inner, join(both, along(both, [(0, 1), (3, 2)])), both)
        yield both
        both = join(both, along(both, [(1, 2), (2, 1)]))
        yield both
        yield jnp.where(inner, both, along(both, [(1, 0), (2, 3)]))


def norm_back(grad_normed, unit, inv_scale, gain):
    scaled = grad_normed * gain
    grad_in = inv_scale * (scaled - unit * jnp.mean(scaled * unit, axis=-1, keepdims=True))
    return (grad_in, jnp.sum(grad_normed * unit, axis=0))


def on_device(
    tokens,
    cotangent,
    segment_ids,
    positions,
    q_weight,
    k_weight,
    v_weight,
    o_weight,
    attn_gain,
    gate_up_weight,
    down_weight,
    mlp_gain,
):
    plane = Plane()
    fast = plane.cube and plane.line
    unit, n = plane.unit, plane.n
    heads = HEADS // n
    share = max(1, n // KV_HEADS)
    q_cols = heads * HEAD
    ff = FF // n
    length = plane.np * tokens.shape[0]

    def qkv_columns(u):
        rows = q_weight.shape[0]
        return jnp.concatenate(
            [
                lax.dynamic_slice(q_weight, (0, u * q_cols), (rows, q_cols)),
                lax.dynamic_slice(k_weight, (0, (u // share) * HEAD), (rows, HEAD)),
                lax.dynamic_slice(v_weight, (0, (u // share) * HEAD), (rows, HEAD)),
            ],
            axis=1,
        )

    def mlp_columns(u, part=0, parts=1):
        rows = gate_up_weight.shape[0] // parts
        return jnp.concatenate(
            [
                lax.dynamic_slice(gate_up_weight, (part * rows, u * ff), (rows, ff)),
                lax.dynamic_slice(gate_up_weight, (part * rows, FF + u * ff), (rows, ff)),
            ],
            axis=1,
        )

    grad_out = cotangent.astype(F32)
    low_out = (RESID * grad_out).astype(BF16)
    gains = jnp.stack([attn_gain, mlp_gain])
    where = jnp.stack([segment_ids, positions])
    w_out = lax.dynamic_slice(o_weight, (plane.p * q_cols, 0), (q_cols, D))
    w_down = lax.dynamic_slice(down_weight, (plane.p * ff, 0), (ff, D))
    if fast:
        crossed = swap(tokens, 2)
        parts = plane.gather_parts(tokens, crossed)
        where = plane.gather_small(where)
        gains = plane.gather_gains(gains)
        w_qkv, arrived = plane.reshard(qkv_columns)
        finish_gate_up = plane.reshard_shared(mlp_columns, (parts[0],) + arrived)
        low_crossed = swap(after(low_out, crossed), 2)
        low_parts = plane.gather_parts(low_out, low_crossed, (parts[1],))
        grad_branch = jnp.concatenate(
            [low_parts[i][j] for i, j in ((0, 0), (1, 0), (0, 1), (1, 1), (2, 0), (3, 0), (2, 1), (3, 1))], axis=0
        )
    else:
        by_group = plane.gather(tokens).reshape(-1, 2, length // 2, D)
        near = by_group.shape[0] // 2
        parts = [by_group[:near, 0], by_group[:near, 1], by_group[near:, 0], by_group[near:, 1]]
        where = plane.gather(where, axis=1)
        gains = lax.all_gather(gains, "fsdp", axis=1, tiled=True)
        w_qkv, _ = plane.reshard(qkv_columns)
        w_gate_up, _ = plane.reshard(mlp_columns)
        grad_branch = plane.gather(low_out)
    gain_one = gains[0].astype(F32)
    gain_two = gains[1].astype(F32)
    segments = where[0].reshape(-1, length)
    places = where[1].reshape(-1, length)
    visible = (
        (segments[:, None, :] == 0) | (segments[:, None, :] == segments[:, :, None])
    ) & (places[:, None, :] <= places[:, :, None])
    visible = visible.astype(F32).reshape(-1, length)
    cosine, sine = rope_tables(places.reshape(-1))

    normed, qkv, attended, tops = attend(
        heads, parts, gain_one[None], w_qkv, cosine, sine, visible
    )
    count = qkv.shape[0]
    flops = 4 * count * length * HEAD * heads

    inputs = tokens.astype(F32)
    if fast:
        far = plane.far_half(attended, w_out, dot)
        total, pieces = plane.near_half(attended, w_out, dot, far)
        w_gate_up = finish_gate_up(pieces[0])
        branch = plane.close(total, pieces)
    else:
        branch = plane.scatter(attended, w_out, dot)
    middle = inputs + RESID * branch
    inv_two = lax.rsqrt(jnp.mean(middle * middle, axis=-1, keepdims=True) + EPS)
    unit_two = middle * inv_two
    low_two = (unit_two * gain_two).astype(BF16)
    normed_mlp = plane.gather(low_two)
    grad_hidden = lax.optimization_barrier(times_t(grad_branch, w_down))

    gate = lax.optimization_barrier(dot(normed_mlp, w_gate_up[:, :ff]))
    up_part = dot(normed_mlp, w_gate_up[:, ff:])
    sigma = jax.nn.sigmoid(gate)
    silu_gate = gate * sigma
    hidden = (silu_gate * up_part).astype(BF16)
    grad_gate = (grad_hidden * up_part * sigma * (1.0 + gate * (1.0 - sigma))).astype(BF16)
    grad_up = (grad_hidden * silu_gate).astype(BF16)
    grad_gate_up = jnp.concatenate([grad_gate, grad_up], axis=1)

    def branch_back(grad_normed_mlp):
        grad_mid_norm, gain_two_grad = norm_back(grad_normed_mlp, unit_two, inv_two, gain_two)
        grad_middle = grad_out + grad_mid_norm
        return grad_middle, gain_two_grad, (RESID * grad_middle).astype(BF16)

    def attention_back(grad_attn_branch):
        grad_attended = times_t(grad_attn_branch, w_out).astype(BF16)
        (grad_lin,) = per_group(
            attend_back_kernel,
            heads,
            length,
            [qkv, cosine, sine, visible, grad_attended],
            [jax.ShapeDtypeStruct(qkv.shape, BF16)],
            "attend_back",
            3 * flops,
        )
        return grad_lin

    inv_one = lax.rsqrt(jnp.mean(inputs * inputs, axis=-1, keepdims=True) + EPS)

    def input_back(grad_normed):
        return norm_back(grad_normed, inputs * inv_one, inv_one, gain_one)

    top_local = jnp.max(tops.reshape(-1, 8, 128), axis=(0, 2))[:heads]
    top_row = jnp.full((1, D), -jnp.inf, F32)
    top_row = lax.dynamic_update_slice(top_row, top_local[None], (0, unit * heads))
    rows = D // n
    shape = (rows, 2 * FF)
    if fast:
        clock = Clock()
        start, keep, tick = clock.start, clock.keep, clock.next
        line = Line(clock, plane.z)
        each = ff // 4

        def down_term(i):
            return outer(hidden[:, i * each : (i + 1) * each], grad_branch).astype(BF16)

        def put(m, sums, into):
            u = plane.unit_of(plane.place ^ m)
            table = jnp.stack([line.inner.astype(jnp.int32), u, n + u])
            return keep(place(table, *sums, into, shape, "place_gate_up"))

        def own_down(sums):
            return keep(plane.to_owner(start(line.pick(*sums))))

        line.step(down_term(0))
        down_next = keep(down_term(1))
        far = keep(plane.far_half(grad_gate_up, w_gate_up, times_t))
        tick()
        line.step(down_next)
        down_next, down_last = keep(down_term(2)), keep(down_term(3))
        grad_mlp = plane.near_half(start(grad_gate_up), w_gate_up, times_t, far)
        keep(grad_mlp[0])
        tick()
        downs = [line.step(down_next)]
        grad_normed_mlp = plane.close(*grad_mlp, clock)
        term = outer(start(normed_mlp), grad_gate_up).astype(BF16).reshape(n, rows, 2 * ff)
        blocks = [keep(plane.block_for(term, m)) for m in range(8)]
        tick()
        downs.append(line.step(down_last))
        for m in (1, 2, 4):
            blocks[m] = keep(swap(start(blocks[m]), m))
        grad_middle, gain_two_grad, low_branch = branch_back(grad_normed_mlp)
        keep(low_branch)
        far = keep(plane.far_half(start(hidden), w_down, dot))
        tick()
        downs.append(line.step(blocks[0]))
        low_branch = start(low_branch)
        near = [low_branch] + [keep(swap(low_branch, m)) for m in ORDER[1:4]]
        branch = plane.near_half(start(hidden), w_down, dot, far)
        keep(branch[0])
        tick()
        downs.append(line.step(blocks[1]))
        near += [swap(start(piece), 1) for piece in near]
        for m in (3, 5):
            blocks[m] = keep(swap(start(blocks[m]), m))
        grad_attn_branch = jnp.concatenate(near, axis=0)
        grad_lin = keep(attention_back(grad_attn_branch))
        tick()
        sums = {0: line.step(blocks[2])}
        blocks[6] = keep(swap(start(blocks[6]), 6))
        o_term = keep(outer(start(attended), grad_attn_branch).astype(BF16))
        far = keep(plane.far_half(start(grad_lin), w_qkv, times_t))
        lin_term = outer(normed, start(grad_lin)).astype(BF16).reshape(n, rows, -1)
        lin_term = keep(jnp.take(lin_term, plane.place ^ jnp.arange(8), axis=0))
        tick()
        sums[1] = line.step(blocks[4])
        blocks[7] = keep(swap(start(blocks[7]), 7))
        lin_far = keep(swap(start(lin_term[1::2]), 1))
        grad_in = plane.near_half(start(grad_lin), w_qkv, times_t, far)
        keep(grad_in[0])
        gate_up_grad = put(0, sums[0], None)
        tick()
        sums[2] = line.step(blocks[3])
        grad_normed = plane.close(*grad_in, clock)
        lin_both = [keep(jnp.stack([start(lin_term[2 * j]), lin_far[j]])) for j in range(4)]
        gate_up_grad = put(1, sums[1], gate_up_grad)
        tick()
        sums[4] = line.step(blocks[5])
        lin_both = lin_both[:1] + [keep(swap(start(lin_both[j]), 2 * j)) for j in (1, 2, 3)]
        grad_in_norm, gain_one_grad = input_back(grad_normed)
        keep(gain_one_grad)
        gate_up_grad = put(2, sums[2], gate_up_grad)
        rounds = plane.total(start(jnp.stack([gain_one_grad, gain_two_grad])), top_row)
        keep(next(rounds))
        tick()
        sums[3] = line.step(blocks[6])
        branch = plane.close(*branch, clock)
        lin_both = keep(jnp.concatenate(lin_both, axis=0))
        gate_up_grad = put(4, sums[4], gate_up_grad)
        keep(next(rounds))
        tick()
        sums[5] = line.step(o_term)
        down_grads = [own_down(downs[0])]
        gate_up_grad = put(3, sums[3], gate_up_grad)
        keep(next(rounds))
        tick()
        sums[6] = line.step(lin_both)
        down_grads.append(own_down(downs[1]))
        gate_up_grad = put(5, sums[5], gate_up_grad)
        keep(next(rounds))
        tick()
        o_sums = line.step(blocks[7])
        down_grads += [own_down(downs[2]), own_down(downs[3])]
        gate_up_grad = put(6, sums[6], gate_up_grad)
        keep(next(rounds))
        tick()
        lin_rows = line.pick(*line.step())
        o_grad = keep(plane.to_owner(start(line.pick(*o_sums)))).astype(F32)
        everything = keep(next(rounds))
        gain_grads, top_row = everything[:2], everything[2:]
        tick()
        last = line.step()
        lin_units = plane.unit_of(plane.place ^ jnp.arange(8))
        down_grad = jnp.concatenate([x.astype(F32) for x in down_grads], axis=0)
        gate_up_grad = put(7, last, gate_up_grad)
    else:
        down_grad = plane.sum_units(outer(hidden, grad_branch)).astype(F32)
        full, units = plane.sum_rows(outer(normed_mlp, grad_gate_up))
        full = plane.in_order(full, units).reshape(rows, n, 2, ff)
        gate_up_grad = jnp.swapaxes(full, 1, 2).reshape(shape).astype(F32)
        grad_normed_mlp = plane.scatter(grad_gate_up, w_gate_up, times_t)
        grad_middle, gain_two_grad, low_branch = branch_back(grad_normed_mlp)
        grad_attn_branch = plane.gather(low_branch)
        grad_lin = attention_back(grad_attn_branch)
        branch = plane.scatter(hidden, w_down, dot)
        grad_normed = plane.scatter(grad_lin, w_qkv, times_t)
        grad_in_norm, gain_one_grad = input_back(grad_normed)
        o_grad = plane.sum_units(outer(attended, grad_attn_branch)).astype(F32)
        lin_rows, lin_units = plane.sum_rows(outer(normed, grad_lin))
        everyone = ("pair", "fsdp", "rep")
        gain_grads = lax.psum(jnp.stack([gain_one_grad, gain_two_grad]), everyone)
        top_row = lax.pmax(top_row, everyone)

    result = (middle + RESID * branch).astype(BF16)
    input_grad = (grad_middle + grad_in_norm).astype(BF16)
    factor = TAU / jnp.maximum(top_row[0, :HEADS], TAU)
    k_factor = jnp.repeat(jnp.min(factor.reshape(KV_HEADS, GROUP), axis=1), HEAD)
    lin_rows = plane.in_order(lin_rows, lin_units).astype(F32)
    q_update = lin_rows[..., :q_cols].reshape(rows, D) * jnp.repeat(factor, HEAD)[None, :]
    kv = lin_rows[..., q_cols:].reshape(rows, n // share, share, 2 * HEAD).sum(axis=2)
    k_update = kv[..., :HEAD].reshape(rows, -1) * k_factor[None, :]
    v_grad = kv[..., HEAD:].reshape(rows, -1)
    gain_grads = lax.dynamic_slice(gain_grads, (0, plane.place * rows), (2, rows))
    return (
        result,
        input_grad,
        q_update,
        k_update,
        v_grad,
        o_grad,
        gain_grads[0],
        gate_up_grad,
        down_grad,
        gain_grads[1],
    )


def solution(mesh):
    tokens = P(("pair", "fsdp", "rep"))
    shard = P("fsdp")
    owned = P(("pair", "fsdp"))
    return jax.shard_map(
        on_device,
        mesh=mesh,
        in_specs=(tokens,) * 4 + (shard,) * 8,
        out_specs=(tokens, tokens) + (owned,) * 8,
        check_vma=False,
    )
```

```python
import jax
import jax.numpy as jnp
from jax import lax
from jax.experimental import pallas as pl
from jax.experimental.pallas import tpu as pltpu
from jax.sharding import PartitionSpec as P

D = 2048
FF = 8192
HEADS = 32
KV_HEADS = 8
HEAD = 64
GROUP = HEADS // KV_HEADS

EPS = 1e-05
THETA = 10000000.0
SCALE = 0.015625
RESID = 0.22
TAU = 3.0

PLANE = ("pair", "fsdp")
F32 = jnp.float32
BF16 = jnp.bfloat16
ORDER = (0, 4, 2, 6, 1, 5, 3, 7)
LAG = 1


def dot(left, right):
    return jnp.dot(left, right, preferred_element_type=F32)


def outer(left, right):
    return lax.dot_general(left, right, (((0,), (0,)), ((), ())), preferred_element_type=F32)


def times_t(left, right):
    return lax.dot_general(left, right, (((1,), (1,)), ((), ())), preferred_element_type=F32)


def swap(x, mask, devices=8):
    return lax.ppermute(x, PLANE, [(i, i ^ mask) for i in range(devices)])


def along(x, pairs):
    return lax.ppermute(x, "rep", pairs)


def after(x, *others):
    return lax.optimization_barrier((x,) + others)[0]


def rope_tables(places):
    half = HEAD // 2
    lane = jnp.arange(2 * HEAD)
    inverse = THETA ** (-((lane % half).astype(F32) * 2.0 / HEAD))
    angle = places.astype(F32)[:, None] * inverse[None, :]
    sign = jnp.where(lane % HEAD < half, -1.0, 1.0)
    return jnp.cos(angle), jnp.sin(angle) * sign[None, :]


def whole_row(cos, sin, heads):
    turned = lax.broadcasted_iota(jnp.int32, cos.shape, 1) < HEAD
    pairs = heads // 2
    cos_row = jnp.concatenate([cos] * pairs + [jnp.where(turned, cos, 1.0)], axis=1)
    sin_row = jnp.concatenate([sin] * pairs + [jnp.where(turned, sin, 0.0)], axis=1)
    return cos_row, sin_row


def half_swap(x):
    width = x.shape[1]
    lane = lax.broadcasted_iota(jnp.int32, x.shape, 1)
    first = (lane & (HEAD - 1)) < HEAD // 2
    return jnp.where(first, pltpu.roll(x, width - HEAD // 2, 1), pltpu.roll(x, HEAD // 2, 1))


def mat_t(left, right):
    return lax.dot_general(left, right, (((1,), (1,)), ((), ())), preferred_element_type=F32)


def mat_tl(left, right):
    return lax.dot_general(left, right, (((0,), (0,)), ((), ())), preferred_element_type=F32)


def attend_kernel(
    heads,
    near,
    first_near,
    second_near,
    first_far,
    second_far,
    gain_ref,
    weight_ref,
    cos_ref,
    sin_ref,
    vis_ref,
    normed_ref,
    qkv_ref,
    att_ref,
    top_ref,
    tokens_ref,
):
    rows = first_near.shape[1]

    @pl.when(pl.program_id(0) < near)
    def _():
        tokens_ref[:rows] = first_near[0]
        tokens_ref[rows:] = second_near[0]

    @pl.when(pl.program_id(0) >= near)
    def _():
        tokens_ref[:rows] = first_far[0]
        tokens_ref[rows:] = second_far[0]

    inputs = tokens_ref[...].astype(F32)
    inv = lax.rsqrt(jnp.mean(inputs * inputs, axis=1, keepdims=True) + EPS)
    normed = (inputs * inv * gain_ref[...]).astype(BF16)
    normed_ref[...] = normed
    x = dot(normed, weight_ref[...])
    cos_row, sin_row = whole_row(cos_ref[...], sin_ref[...], heads)
    row = (x * cos_row + half_swap(x) * sin_row).astype(BF16)
    qkv_ref[...] = row
    key = row[:, heads * HEAD : (heads + 1) * HEAD]
    value = row[:, (heads + 1) * HEAD :]
    visible = vis_ref[...] > 0.0
    top_ref[...] = jnp.full(top_ref.shape, -jnp.inf, F32)
    outs = []
    for h in range(heads):
        scores = mat_t(row[:, h * HEAD : (h + 1) * HEAD], key) * SCALE
        scores = jnp.where(visible, scores, -jnp.inf)
        peak = jnp.max(scores, axis=1, keepdims=True)
        grown = jnp.exp(scores - peak)
        probs = (grown / jnp.sum(grown, axis=1, keepdims=True)).astype(BF16)
        outs.append(dot(probs, value).astype(BF16))
        top_ref[h : h + 1, :] = jnp.broadcast_to(jnp.max(peak, axis=0, keepdims=True), (1, 128))
    att_ref[...] = jnp.concatenate(outs, axis=1)


def attend(heads, parts, gain, weight, cosine, sine, visible):
    near = parts[0].shape[0]
    groups = near + parts[2].shape[0]
    length = parts[0].shape[1] + parts[1].shape[1]
    width = weight.shape[1]

    def part(x, is_near):
        block = (1,) + x.shape[1:]
        if is_near:
            return pl.BlockSpec(block, lambda g: (jnp.minimum(g, near - 1), 0, 0))
        return pl.BlockSpec(block, lambda g: (jnp.maximum(g - near, 0), 0, 0))

    def whole(x):
        return pl.BlockSpec(x.shape, lambda g: (0, 0))

    def rows(columns, each=length):
        return pl.BlockSpec((each, columns), lambda g: (g, 0))

    total = groups * length
    return pl.pallas_call(
        lambda *refs: attend_kernel(heads, near, *refs),
        grid=(groups,),
        in_specs=[part(x, i < 2) for i, x in enumerate(parts)]
        + [whole(gain), whole(weight), rows(cosine.shape[1]), rows(sine.shape[1]), rows(visible.shape[1])],
        out_specs=[rows(D), rows(width), rows(heads * HEAD), rows(128, 8)],
        out_shape=[
            jax.ShapeDtypeStruct((total, D), BF16),
            jax.ShapeDtypeStruct((total, width), BF16),
            jax.ShapeDtypeStruct((total, heads * HEAD), BF16),
            jax.ShapeDtypeStruct((8 * groups, 128), F32),
        ],
        scratch_shapes=[pltpu.VMEM((length, D), BF16)],
        name="attend",
        cost_estimate=pl.CostEstimate(
            flops=2 * total * D * width, bytes_accessed=8 * total * D, transcendentals=0
        ),
    )(*parts, gain, weight, cosine, sine, visible)


def attend_back_kernel(heads, qkv_ref, cos_ref, sin_ref, vis_ref, grad_ref, out_ref):
    row = qkv_ref[...]
    key = row[:, heads * HEAD : (heads + 1) * HEAD]
    value = row[:, (heads + 1) * HEAD :]
    visible = vis_ref[...] > 0.0
    grad_att = grad_ref[...]
    grads = []
    grad_key = jnp.zeros((row.shape[0], HEAD), F32)
    grad_value = jnp.zeros((row.shape[0], HEAD), F32)
    for h in range(heads):
        query = row[:, h * HEAD : (h + 1) * HEAD]
        grad_h = grad_att[:, h * HEAD : (h + 1) * HEAD]
        scores = jnp.where(visible, mat_t(query, key) * SCALE, -jnp.inf)
        peak = jnp.max(scores, axis=1, keepdims=True)
        grown = jnp.exp(scores - peak)
        probs = grown / jnp.sum(grown, axis=1, keepdims=True)
        grad_probs = mat_t(grad_h, value)
        delta = jnp.sum(probs * grad_probs, axis=1, keepdims=True)
        grad_scores = (probs * (grad_probs - delta) * SCALE).astype(BF16)
        grads.append(dot(grad_scores, key))
        grad_key = grad_key + mat_tl(grad_scores, query)
        grad_value = grad_value + mat_tl(probs.astype(BF16), grad_h)
    x = jnp.concatenate(grads + [grad_key, grad_value], axis=1)
    cos_row, sin_row = whole_row(cos_ref[...], sin_ref[...], heads)
    out_ref[...] = (x * cos_row - half_swap(x) * sin_row).astype(BF16)


def per_group(kernel, heads, length, ins, outs, name, flops):
    groups = ins[0].shape[0] // length

    def spec(x):
        rows = x.shape[0] // groups
        return pl.BlockSpec((rows, x.shape[1]), lambda g: (g, 0))

    return pl.pallas_call(
        lambda *refs: kernel(heads, *refs),
        grid=(groups,),
        in_specs=[spec(x) for x in ins],
        out_specs=[spec(x) for x in outs],
        out_shape=outs,
        name=name,
        cost_estimate=pl.CostEstimate(
            flops=flops, bytes_accessed=4 * sum(x.size for x in ins), transcendentals=0
        ),
    )(*ins)


def place_kernel(table, sum_ref, copy_ref, *refs):
    out_ref = refs[-1]

    @pl.when(table[0] == 1)
    def _():
        out_ref[...] = sum_ref[0].astype(F32)

    @pl.when(table[0] == 0)
    def _():
        out_ref[...] = copy_ref[0].astype(F32)


def place(table, summed, copied, into, shape, name):
    count, rows, width = summed.shape
    columns = width // 2
    piece = pl.BlockSpec((1, rows, columns), lambda b, i, t: (b, 0, i))
    in_specs = [piece, piece]
    args = [summed, copied]
    aliases = {}
    if into is not None:
        in_specs.append(pl.BlockSpec(memory_space=pl.ANY))
        args.append(into)
        aliases = {3: 0}
    return pl.pallas_call(
        place_kernel,
        grid_spec=pltpu.PrefetchScalarGridSpec(
            num_scalar_prefetch=1,
            grid=(count, 2),
            in_specs=in_specs,
            out_specs=pl.BlockSpec((rows, columns), lambda b, i, t: (0, t[1 + 2 * b + i])),
        ),
        out_shape=jax.ShapeDtypeStruct(shape, F32),
        input_output_aliases=aliases,
        name=name,
        cost_estimate=pl.CostEstimate(
            flops=0, bytes_accessed=8 * count * rows * width, transcendentals=0
        ),
    )(table, *args)


class Clock:
    def __init__(self):
        self.kept = []
        self.past = []

    def start(self, x):
        if len(self.past) < LAG:
            return x
        return after(x, *self.past[-LAG])

    def keep(self, x):
        self.kept.append(x)
        return x

    def next(self):
        self.past.append(tuple(self.kept))
        self.kept = []


class Line:
    def __init__(self, clock, z):
        self.clock = clock
        self.inner = (z == 1) | (z == 2)
        self.across = None
        self.back = None

    def send(self, arrays, pairs):
        arrays = [self.clock.start(x) for x in arrays]
        return arrays, [self.clock.keep(along(x, pairs)) for x in arrays]

    def step(self, chunk=None):
        total, self.back = self.back, None
        middle, self.across = self.across, None
        out, home = [(0, 1), (3, 2)], [(1, 0), (2, 3)]
        done = got = ()
        if total and chunk and [x.shape for x in total] == [x.shape for x in chunk]:
            mixed = [jnp.where(self.inner, x, y) for x, y in zip(total, chunk)]
            done, got = self.send(mixed, out + home)
            self.across = [x + y for x, y in zip(chunk, got)]
        else:
            if chunk:
                chunk, more = self.send(chunk, out)
                self.across = [x + y for x, y in zip(chunk, more)]
            if total:
                done, got = self.send(total, home)
        if middle:
            middle, more = self.send(middle, [(1, 2), (2, 1)])
            self.back = [x + y for x, y in zip(middle, more)]
        return list(zip(done, got))

    def pick(self, summed, copied):
        return jnp.where(self.inner, summed, copied)


class Plane:
    def __init__(self):
        self.np = lax.axis_size("pair")
        self.nf = lax.axis_size("fsdp")
        self.nr = lax.axis_size("rep")
        self.n = self.np * self.nf
        self.p = lax.axis_index("pair")
        self.f = lax.axis_index("fsdp")
        self.z = lax.axis_index("rep")
        self.place = self.p * self.nf + self.f
        self.unit = self.np * self.f + self.p
        self.cube = self.np == 2 and self.nf == 4
        self.line = self.nr == 4

    def gather(self, x, axis=0):
        if not self.cube:
            full = lax.all_gather(x, PLANE, axis=axis, tiled=True)
            return self.to_groups(full, axis)
        near = [x] + [swap(x, m) for m in ORDER[1:4]]
        far = [swap(piece, 1) for piece in near]
        return jnp.concatenate(near + far, axis=axis)

    def gather_parts(self, x, swapped, hold=()):
        two = jnp.stack([x, swapped])
        other = swap(after(two, *hold), 4)
        return two, other, swap(after(two, other), 1), swap(other, 1)

    def gather_small(self, x):
        pair = jnp.concatenate([x, swap(x, 4)], axis=1)
        quad = jnp.concatenate([pair, swap(pair, 2)], axis=1)
        return jnp.concatenate([quad, swap(quad, 1)], axis=1)

    def gather_gains(self, x):
        for k in (1, 2):
            other = swap(x, k)
            odd = (self.f & k) > 0
            x = jnp.concatenate([jnp.where(odd, other, x), jnp.where(odd, x, other)], axis=1)
        return x

    def to_groups(self, x, axis=0):
        shape = x.shape
        y = x.reshape(shape[:axis] + (self.np, self.nf, -1) + shape[axis + 1 :])
        return jnp.swapaxes(y, axis, axis + 1).reshape(shape)

    def from_groups(self, x):
        y = x.reshape((self.nf, self.np, -1) + x.shape[1:])
        return jnp.swapaxes(y, 0, 1).reshape(x.shape)

    def scatter(self, left, right, product):
        if not self.cube:
            whole = self.from_groups(product(left, right).astype(BF16))
            return lax.psum_scatter(whole, PLANE, scatter_dimension=0, tiled=True).astype(F32)
        return self.close(*self.near_half(left, right, product, self.far_half(left, right, product)))

    def far_half(self, left, right, product):
        return swap(product(left[left.shape[0] // 2 :], right).astype(BF16), 1)

    def near_half(self, left, right, product, far):
        half = left.shape[0] // 2
        size = half // 4
        near = product(left[:half], right) + far.astype(F32)
        return near[:size], [near[i * size : (i + 1) * size].astype(BF16) for i in (1, 2, 3)]

    def close(self, total, pieces, clock=None):
        got = []
        for i, piece in enumerate(pieces):
            got.append(swap(clock.start(piece) if clock else piece, ORDER[i + 1]))
        for piece in got:
            if clock:
                clock.keep(piece)
            total = total + piece.astype(F32)
        return total

    def reshard(self, columns):
        if not self.cube:
            parts = jnp.stack([columns(self.np * i + self.p) for i in range(self.nf)])
            got = lax.all_to_all(parts, "fsdp", 0, 0, tiled=True)
            return got.reshape((-1,) + got.shape[2:]), ()
        own = columns(self.unit)
        rows = own.shape[0]
        got = [swap(columns(self.np * (self.f ^ k) + self.p), k) for k in (2, 3)]
        got = [swap(columns(after(self.np * (self.f ^ 1) + self.p, *got)), 1)] + got
        out = jnp.zeros((self.nf * rows,) + own.shape[1:], own.dtype)
        out = lax.dynamic_update_slice(out, own, (self.f * rows, 0))
        for k, piece in zip((1, 2, 3), got):
            out = lax.dynamic_update_slice(out, piece, ((self.f ^ k) * rows, 0))
        return out, tuple(got[1:])

    def reshard_shared(self, columns, first):
        got = []
        for k in (2, 3):
            got.append(swap(columns(after(self.np * (self.f ^ k) + self.p, *first), self.z, 4), k))
        sides = self.line_sides(jnp.stack(got))

        def finish(hold):
            zero = after(jnp.zeros((), BF16), hold)
            own = columns(after(self.unit, hold), 0, 1)
            rows, width = own.shape
            quarter = rows // 4
            near = swap(columns(after(self.np * (self.f ^ 1) + self.p, hold), 0, 1), 1)
            shards = sides + self.line_rest(*[after(side, hold) for side in sides[1:]])
            out = jnp.broadcast_to(zero, (self.nf * rows, width))
            out = lax.dynamic_update_slice(out, own, (self.f * rows, 0))
            out = lax.dynamic_update_slice(out, near, ((self.f ^ 1) * rows, 0))
            for shard, where in reversed(list(zip(shards, self.line_shards()))):
                for i, k in enumerate((2, 3)):
                    start = (self.f ^ k) * rows + where * quarter
                    out = lax.dynamic_update_slice(out, shard[i], (start, 0))
            return out

        return finish, tuple(got)

    def line_shards(self):
        z = self.z
        return (
            z,
            jnp.maximum(z - 1, 0),
            jnp.minimum(z + 1, 3),
            jnp.where(z < 2, z + 2, z - 2),
            jnp.where(z == 0, 3, jnp.where(z == 3, 0, z)),
        )

    def line_sides(self, own):
        right = along(own, [(0, 1), (1, 2), (2, 3)])
        return own, right, along(own, [(1, 0), (2, 1), (3, 2)])

    def line_rest(self, right, left):
        two = jnp.where(
            self.z < 2, along(left, [(1, 0), (2, 1)]), along(right, [(1, 2), (2, 3)])
        )
        return two, along(two, [(2, 3), (1, 0)])

    def unit_of(self, place):
        return self.np * (place % self.nf) + place // self.nf

    def to_owner(self, x):
        pairs = []
        for p in range(self.np):
            for f in range(self.nf):
                pairs.append((p * self.nf + f, self.np * f + p))
        moved = lax.ppermute(x, PLANE, [pair for pair in pairs if pair[0] != pair[1]])
        return jnp.where(self.place == self.unit, x, moved)

    def sum_rows(self, term):
        rows, width = term.shape
        each = rows // (self.n * self.nr)
        split = term.astype(BF16).reshape(self.n, self.nr, each, width)
        mine = lax.psum_scatter(jnp.swapaxes(split, 0, 1), "rep", scatter_dimension=0)
        moved = lax.all_to_all(mine, PLANE, 0, 0, tiled=True)
        full = jnp.swapaxes(lax.all_gather(moved, "rep", axis=0), 0, 1)
        return full.reshape(self.n, -1, width), self.unit_of(jnp.arange(self.n))

    def in_order(self, full, units):
        inverse = jnp.zeros((self.n,), jnp.int32).at[units].set(jnp.arange(self.n, dtype=jnp.int32))
        return jnp.swapaxes(jnp.take(full, inverse, axis=0), 0, 1)

    def sum_units(self, term):
        mine = lax.psum_scatter(term.astype(BF16), "rep", scatter_dimension=0, tiled=True)
        return lax.all_gather(self.to_owner(mine), "rep", axis=0, tiled=True)

    def block_for(self, split, m):
        return lax.dynamic_index_in_dim(split, self.place ^ m, 0, keepdims=False)

    def total(self, sums, top):
        count = sums.shape[0]
        both = jnp.concatenate([sums, top], axis=0)

        def join(a, b):
            return jnp.concatenate(
                [a[:count] + b[:count], jnp.maximum(a[count:], b[count:])], axis=0
            )

        for m in (1, 2, 4):
            both = join(both, swap(both, m))
            yield both
        inner = (self.z == 1) | (self.z == 2)
        both = jnp.where(inner, join(both, along(both, [(0, 1), (3, 2)])), both)
        yield both
        both = join(both, along(both, [(1, 2), (2, 1)]))
        yield both
        yield jnp.where(inner, both, along(both, [(1, 0), (2, 3)]))


def norm_back(grad_normed, unit, inv_scale, gain):
    scaled = grad_normed * gain
    grad_in = inv_scale * (scaled - unit * jnp.mean(scaled * unit, axis=-1, keepdims=True))
    return (grad_in, jnp.sum(grad_normed * unit, axis=0))


def on_device(
    tokens,
    cotangent,
    segment_ids,
    positions,
    q_weight,
    k_weight,
    v_weight,
    o_weight,
    attn_gain,
    gate_up_weight,
    down_weight,
    mlp_gain,
):
    plane = Plane()
    fast = plane.cube and plane.line
    unit, n = plane.unit, plane.n
    heads = HEADS // n
    share = max(1, n // KV_HEADS)
    q_cols = heads * HEAD
    ff = FF // n
    length = plane.np * tokens.shape[0]

    def qkv_columns(u):
        rows = q_weight.shape[0]
        return jnp.concatenate(
            [
                lax.dynamic_slice(q_weight, (0, u * q_cols), (rows, q_cols)),
                lax.dynamic_slice(k_weight, (0, (u // share) * HEAD), (rows, HEAD)),
                lax.dynamic_slice(v_weight, (0, (u // share) * HEAD), (rows, HEAD)),
            ],
            axis=1,
        )

    def mlp_columns(u, part=0, parts=1):
        rows = gate_up_weight.shape[0] // parts
        return jnp.concatenate(
            [
                lax.dynamic_slice(gate_up_weight, (part * rows, u * ff), (rows, ff)),
                lax.dynamic_slice(gate_up_weight, (part * rows, FF + u * ff), (rows, ff)),
            ],
            axis=1,
        )

    grad_out = cotangent.astype(F32)
    low_out = (RESID * grad_out).astype(BF16)
    gains = jnp.stack([attn_gain, mlp_gain])
    where = jnp.stack([segment_ids, positions])
    w_out = lax.dynamic_slice(o_weight, (plane.p * q_cols, 0), (q_cols, D))
    w_down = lax.dynamic_slice(down_weight, (plane.p * ff, 0), (ff, D))
    if fast:
        crossed = swap(tokens, 2)
        parts = plane.gather_parts(tokens, crossed)
        where = plane.gather_small(where)
        gains = plane.gather_gains(gains)
        w_qkv, arrived = plane.reshard(lambda u: qkv_columns(after(u, parts[0])))
        finish_gate_up, quarters = plane.reshard_shared(mlp_columns, (parts[0],))
        w_qkv = after(w_qkv, *quarters)
        low_swapped = swap(after(low_out, parts[1]), 4)
        w_qkv = after(w_qkv, low_swapped)
        low_pair = jnp.stack([low_out, low_swapped])
        low_other = swap(after(low_pair, *quarters), 2)
    else:
        by_group = plane.gather(tokens).reshape(-1, 2, length // 2, D)
        near = by_group.shape[0] // 2
        parts = [by_group[:near, 0], by_group[:near, 1], by_group[near:, 0], by_group[near:, 1]]
        where = plane.gather(where, axis=1)
        gains = lax.all_gather(gains, "fsdp", axis=1, tiled=True)
        w_qkv, _ = plane.reshard(qkv_columns)
        w_gate_up, _ = plane.reshard(mlp_columns)
        grad_branch = plane.gather(low_out)
    gain_one = gains[0].astype(F32)
    gain_two = gains[1].astype(F32)
    segments = where[0].reshape(-1, length)
    places = where[1].reshape(-1, length)
    visible = (
        (segments[:, None, :] == 0) | (segments[:, None, :] == segments[:, :, None])
    ) & (places[:, None, :] <= places[:, :, None])
    visible = visible.astype(F32).reshape(-1, length)
    cosine, sine = rope_tables(places.reshape(-1))

    normed, qkv, attended, tops = attend(
        heads, parts, gain_one[None], w_qkv, cosine, sine, visible
    )
    count = qkv.shape[0]
    flops = 4 * count * length * HEAD * heads

    inputs = tokens.astype(F32)
    if fast:
        far = plane.far_half(attended, w_out, dot)
        total, pieces = plane.near_half(attended, w_out, dot, far)
        w_gate_up = finish_gate_up(pieces[0])
        branch = plane.close(total, pieces)
    else:
        branch = plane.scatter(attended, w_out, dot)
    middle = inputs + RESID * branch
    inv_two = lax.rsqrt(jnp.mean(middle * middle, axis=-1, keepdims=True) + EPS)
    unit_two = middle * inv_two
    low_two = (unit_two * gain_two).astype(BF16)
    normed_mlp = plane.gather(low_two)
    if fast:
        low_parts = [after(low_pair, *pieces), after(low_other, *pieces)]
        low_parts += [swap(part, 1) for part in low_parts]
        grad_branch = jnp.concatenate([part.reshape(-1, D) for part in low_parts], axis=0)
    grad_hidden = lax.optimization_barrier(times_t(grad_branch, w_down))

    gate = lax.optimization_barrier(dot(normed_mlp, w_gate_up[:, :ff]))
    up_part = dot(normed_mlp, w_gate_up[:, ff:])
    sigma = jax.nn.sigmoid(gate)
    silu_gate = gate * sigma
    hidden = (silu_gate * up_part).astype(BF16)
    grad_gate = (grad_hidden * up_part * sigma * (1.0 + gate * (1.0 - sigma))).astype(BF16)
    grad_up = (grad_hidden * silu_gate).astype(BF16)
    grad_gate_up = jnp.concatenate([grad_gate, grad_up], axis=1)

    def branch_back(grad_normed_mlp):
        grad_mid_norm, gain_two_grad = norm_back(grad_normed_mlp, unit_two, inv_two, gain_two)
        grad_middle = grad_out + grad_mid_norm
        return grad_middle, gain_two_grad, (RESID * grad_middle).astype(BF16)

    def attention_back(grad_attn_branch):
        grad_attended = times_t(grad_attn_branch, w_out).astype(BF16)
        (grad_lin,) = per_group(
            attend_back_kernel,
            heads,
            length,
            [qkv, cosine, sine, visible, grad_attended],
            [jax.ShapeDtypeStruct(qkv.shape, BF16)],
            "attend_back",
            3 * flops,
        )
        return grad_lin

    inv_one = lax.rsqrt(jnp.mean(inputs * inputs, axis=-1, keepdims=True) + EPS)

    def input_back(grad_normed):
        return norm_back(grad_normed, inputs * inv_one, inv_one, gain_one)

    top_local = jnp.max(tops.reshape(-1, 8, 128), axis=(0, 2))[:heads]
    top_row = jnp.full((1, D), -jnp.inf, F32)
    top_row = lax.dynamic_update_slice(top_row, top_local[None], (0, unit * heads))
    rows = D // n
    shape = (rows, 2 * FF)
    if fast:
        clock = Clock()
        start, keep, tick = clock.start, clock.keep, clock.next
        line = Line(clock, plane.z)
        each = ff // 2

        def down_term(i):
            columns = hidden[:, i * each : (i + 1) * each]
            return outer(start(columns), grad_branch).astype(BF16)

        def put(pair, sums, into):
            units = [plane.unit_of(plane.place ^ m) for m in pair]
            table = jnp.stack([line.inner.astype(jnp.int32)] + [i * n + u for u in units for i in (0, 1)])
            return keep(place(table, *sums[0], into, shape, "place_gate_up"))

        def own_rows(sums):
            return keep(plane.to_owner(start(line.pick(*sums))))

        def both(pair):
            return [jnp.stack([blocks[m] for m in pair])]

        down_first = down_term(0)
        line.step([down_first])
        grad_gate_up = after(grad_gate_up, down_first)
        down_next = keep(down_term(1))
        far = plane.far_half(grad_gate_up, w_gate_up, times_t)
        grad_mlp = plane.near_half(grad_gate_up, w_gate_up, times_t, far)
        grad_normed_mlp = plane.close(*grad_mlp, clock)
        late = after(normed_mlp, grad_mlp[1][0])
        term = outer(late, grad_gate_up).astype(BF16).reshape(n, rows, 2 * ff)
        blocks = [keep(plane.block_for(term, m)) for m in range(8)]
        blocks[1] = keep(swap(blocks[1], 1))
        tick()
        line.step([down_next])
        grad_middle, gain_two_grad, low_branch = branch_back(grad_normed_mlp)
        near = [low_branch] + [swap(low_branch, m) for m in ORDER[1:4]]
        near += [keep(swap(piece, 1)) for piece in near]
        late = after(start(hidden), low_branch)
        branch = plane.near_half(late, w_down, dot, plane.far_half(late, w_down, dot))
        keep(branch[0])
        tick()
        downs = line.step(both((0, 1)))
        for m in (2, 4):
            blocks[m] = keep(swap(start(blocks[m]), m))
        grad_attn_branch = start(jnp.concatenate(near, axis=0))
        grad_lin = attention_back(grad_attn_branch)
        grad_in = plane.near_half(grad_lin, w_qkv, times_t, plane.far_half(grad_lin, w_qkv, times_t))
        keep(grad_in[0])
        lin_term = outer(normed, grad_lin).astype(BF16).reshape(n, rows, -1)
        lin_term = keep(jnp.take(lin_term, plane.place ^ jnp.arange(8), axis=0))
        o_term = keep(outer(attended, after(grad_attn_branch, lin_term)).astype(BF16))
        tick()
        downs += line.step(both((2, 4)))
        grad_normed = plane.close(*grad_in, clock)
        for m in (3, 5):
            blocks[m] = keep(swap(after(start(blocks[m]), grad_normed), m))
        lin_far = keep(swap(start(lin_term[1::2]), 1))
        tick()
        first = line.step(both((3, 5)))
        lin_both = [jnp.stack([lin_term[2 * j], lin_far[j]]) for j in range(4)]
        lin_both = lin_both[:1] + [keep(swap(start(lin_both[j]), 2 * j)) for j in (1, 2, 3)]
        blocks[6] = keep(swap(after(start(blocks[6]), *lin_both[1:]), 6))
        grad_in_norm, gain_one_grad = input_back(start(grad_normed))
        rounds = plane.total(jnp.stack([gain_one_grad, gain_two_grad]), top_row)
        keep(next(rounds))
        tick()
        second = line.step([o_term, jnp.concatenate(lin_both, axis=0)])
        blocks[7] = keep(swap(start(blocks[7]), 7))
        gate_up_grad = put((0, 1), first, None)
        next(rounds)
        keep(next(rounds))
        tick()
        third = line.step(both((6, 7)))
        gate_up_grad = put((2, 4), second, gate_up_grad)
        down_grads = [own_rows(downs[0])]
        keep(next(rounds))
        tick()
        mixed = line.step()
        gate_up_grad = put((3, 5), third, gate_up_grad)
        down_grads.append(own_rows(downs[1]))
        keep(next(rounds))
        everything = keep(next(rounds))
        gain_grads, top_row = everything[:2], everything[2:]
        tick()
        last = line.step()
        branch = plane.close(*branch, clock)
        o_grad = own_rows(mixed[0]).astype(F32)
        lin_rows = line.pick(*mixed[1])
        lin_units = plane.unit_of(plane.place ^ jnp.arange(8))
        down_grad = jnp.concatenate([x.astype(F32) for x in down_grads], axis=0)
        gate_up_grad = put((6, 7), last, gate_up_grad)
    else:
        down_grad = plane.sum_units(outer(hidden, grad_branch)).astype(F32)
        full, units = plane.sum_rows(outer(normed_mlp, grad_gate_up))
        full = plane.in_order(full, units).reshape(rows, n, 2, ff)
        gate_up_grad = jnp.swapaxes(full, 1, 2).reshape(shape).astype(F32)
        grad_normed_mlp = plane.scatter(grad_gate_up, w_gate_up, times_t)
        grad_middle, gain_two_grad, low_branch = branch_back(grad_normed_mlp)
        grad_attn_branch = plane.gather(low_branch)
        grad_lin = attention_back(grad_attn_branch)
        branch = plane.scatter(hidden, w_down, dot)
        grad_normed = plane.scatter(grad_lin, w_qkv, times_t)
        grad_in_norm, gain_one_grad = input_back(grad_normed)
        o_grad = plane.sum_units(outer(attended, grad_attn_branch)).astype(F32)
        lin_rows, lin_units = plane.sum_rows(outer(normed, grad_lin))
        everyone = ("pair", "fsdp", "rep")
        gain_grads = lax.psum(jnp.stack([gain_one_grad, gain_two_grad]), everyone)
        top_row = lax.pmax(top_row, everyone)

    result = (middle + RESID * branch).astype(BF16)
    input_grad = (grad_middle + grad_in_norm).astype(BF16)
    factor = TAU / jnp.maximum(top_row[0, :HEADS], TAU)
    k_factor = jnp.repeat(jnp.min(factor.reshape(KV_HEADS, GROUP), axis=1), HEAD)
    lin_rows = plane.in_order(lin_rows, lin_units).astype(F32)
    q_update = lin_rows[..., :q_cols].reshape(rows, D) * jnp.repeat(factor, HEAD)[None, :]
    kv = lin_rows[..., q_cols:].reshape(rows, n // share, share, 2 * HEAD).sum(axis=2)
    k_update = kv[..., :HEAD].reshape(rows, -1) * k_factor[None, :]
    v_grad = kv[..., HEAD:].reshape(rows, -1)
    gain_grads = lax.dynamic_slice(gain_grads, (0, plane.place * rows), (2, rows))
    return (
        result,
        input_grad,
        q_update,
        k_update,
        v_grad,
        o_grad,
        gain_grads[0],
        gate_up_grad,
        down_grad,
        gain_grads[1],
    )


def solution(mesh):
    tokens = P(("pair", "fsdp", "rep"))
    shard = P("fsdp")
    owned = P(("pair", "fsdp"))
    return jax.shard_map(
        on_device,
        mesh=mesh,
        in_specs=(tokens,) * 4 + (shard,) * 8,
        out_specs=(tokens, tokens) + (owned,) * 8,
        check_vma=False,
    )
```
